32 devices in a mesh: dp: 32 (over z, y, x, core).
Axes of the slice: x: 2, y: 2, z: 4, core: 2. Of those that a mesh axis runs over, the one named last changes fastest.
Arguments:
- series: bfloat16 [32, 288, 512], P('dp'), may hold values from -6 to 6
- horizon: int32 [32], P('dp'), may hold values from 0 to 3
- cotangent: bfloat16 [32, 288, 512], P('dp'), may hold values from -6 to 6
- fine_down: bfloat16 [12, 262144], replicated, may hold values from -0.078125 to 0.078125
- fine_down_bias: bfloat16 [512], replicated, may hold values from -3 to 3
- fine_isometric: bfloat16 [25, 262144], replicated, may hold values from -0.0546875 to 0.0546875
- fine_isometric_bias: bfloat16 [512], replicated, may hold values from -3 to 3
- fine_upsample: bfloat16 [12, 262144], replicated, may hold values from -0.25 to 0.25
- fine_upsample_bias: bfloat16 [512], replicated, may hold values from -3 to 3
- coarse_down: bfloat16 [16, 262144], replicated, may hold values from -0.0625 to 0.0625
- coarse_down_bias: bfloat16 [512], replicated, may hold values from -3 to 3
- coarse_isometric: bfloat16 [19, 262144], replicated, may hold values from -0.0625 to 0.0625
- coarse_isometric_bias: bfloat16 [512], replicated, may hold values from -3 to 3
- coarse_upsample: bfloat16 [16, 262144], replicated, may hold values from -0.25 to 0.25
- coarse_upsample_bias: bfloat16 [512], replicated, may hold values from -3 to 3
- branch_gain: bfloat16 [512], replicated, may hold values from 0.099609375 to 1.8984375
- branch_bias: bfloat16 [512], replicated, may hold values from -3 to 3
- merge_weight: bfloat16 [2, 262144], replicated, may hold values from -0.1875 to 0.1875
- merge_bias: bfloat16 [512], replicated, may hold values from -3 to 3
- first_gain: bfloat16 [512], replicated, may hold values from 0.099609375 to 1.8984375
- first_bias: bfloat16 [512], replicated, may hold values from -3 to 3
- expand_weight: bfloat16 [512, 2048], replicated, may hold values from -0.25 to 0.25
- expand_bias: bfloat16 [2048], replicated, may hold values from -3 to 3
- reduce_weight: bfloat16 [2048, 512], replicated, may hold values from -0.125 to 0.125
- reduce_bias: bfloat16 [512], replicated, may hold values from -3 to 3
- final_gain: bfloat16 [512], replicated, may hold values from 0.099609375 to 1.8984375
- final_bias: bfloat16 [512], replicated, may hold values from -3 to 3
Outputs:
- result: float32 [32, 288, 512], P('dp')
- series_gradient: float32 [32, 288, 512], P('dp')
- fine_down_gradient: float32 [12, 262144], P(None, 'dp')
- fine_down_bias_gradient: float32 [512], replicated
- fine_isometric_gradient: float32 [25, 262144], P(None, 'dp')
- fine_isometric_bias_gradient: float32 [512], replicated
- fine_upsample_gradient: float32 [12, 262144], P(None, 'dp')
- fine_upsample_bias_gradient: float32 [512], replicated
- coarse_down_gradient: float32 [16, 262144], P(None, 'dp')
- coarse_down_bias_gradient: float32 [512], replicated
- coarse_isometric_gradient: float32 [19, 262144], P(None, 'dp')
- coarse_isometric_bias_gradient: float32 [512], replicated
- coarse_upsample_gradient: float32 [16, 262144], P(None, 'dp')
- coarse_upsample_bias_gradient: float32 [512], replicated
- branch_gain_gradient: float32 [512], replicated
- branch_bias_gradient: float32 [512], replicated
- merge_weight_gradient: float32 [2, 262144], P(None, 'dp')
- merge_bias_gradient: float32 [512], replicated
- first_gain_gradient: float32 [512], replicated
- first_bias_gradient: float32 [512], replicated
- expand_weight_gradient: float32 [512, 2048], P(None, 'dp')
- expand_bias_gradient: float32 [2048], replicated
- reduce_weight_gradient: float32 [2048, 512], P('dp')
- reduce_bias_gradient: float32 [512], replicated
- final_gain_gradient: float32 [512], replicated
- final_bias_gradient: float32 [512], replicated
The draws below stay inside these ranges and needn't reach their ends.
Inputs may be any that keep to these rules, and one draw needn't show every extreme that they name: A series' valid steps are the first 288 * (192, 288, 432, 816)[horizon] / 816.
All inputs are finite; a program needn't handle non-finite values.
Results may differ from the reference program's by a relative error of at most 0.014.
Values may be sent and summed in bfloat16 or wider, within the bound.
A program may use at most 384 MiB of HBM per device.

```python
import jax
import jax.numpy as jnp
from jax import lax

D = 512
FF = 2048
K_A = 12
K_B = 16
LEN = 288
SERIES = 32
ISO_A = 25
ISO_B = 19


def plant(values, rng, low, high):
    spot = [jax.random.randint(jax.random.fold_in(rng, axis), (), 0, length) for axis, length in enumerate(values.shape)]
    main_axis = values.shape.index(max(values.shape))
    neighbour = spot[:main_axis] + [(spot[main_axis] + 1) % values.shape[main_axis]] + spot[main_axis + 1:]
    return values.at[tuple(spot)].set(low).at[tuple(neighbour)].set(high)


def levels(key, extent, pieces, low, largest):
    level = 1.0
    for position, parts in pieces:
        draws = jax.random.uniform(jax.random.fold_in(jax.random.fold_in(key, 6), position), (parts,), jnp.float32, low / len(pieces), largest / len(pieces))
        level = level * jnp.repeat(jnp.exp(draws), extent[position] // parts).reshape((-1,) + (1,) * (len(extent) - 1 - position))
    return level


def bell_draw(stream_key, dims, width, reach, split=(), kind=jnp.bfloat16):
    values = jax.random.normal(stream_key, dims, jnp.float32) * width
    if len(split) > 0:
        values = levels(stream_key, dims, split, -0.22, 0.18) * values
    return jnp.clip(values, min=-reach, max=reach).astype(kind)


def setup_inputs(seed: int = 0) -> dict:
    key_list = jax.random.split(jax.random.key(seed), 28)
    series = bell_draw(key_list[0], (SERIES, LEN, D), 1.0, 6.0, ((0, 32),))
    horizon = plant(jax.random.randint(key_list[1], (SERIES,), 0, 4), jax.random.fold_in(key_list[1], 1), 0, 3).astype(jnp.int32)
    cotangent = bell_draw(key_list[2], (SERIES, LEN, D), 1.0, 6.0, ((0, 32),))
    fine_down = bell_draw(key_list[3], (K_A, D * D), (K_A * D) ** -0.5, 0.078125)
    fine_down_bias = bell_draw(key_list[4], (D,), 0.3, 3.0)
    fine_isometric = bell_draw(key_list[5], (ISO_A, D * D), (ISO_A * D) ** -0.5, 0.0546875)
    fine_isometric_bias = bell_draw(key_list[6], (D,), 0.3, 3.0)
    fine_upsample = bell_draw(key_list[7], (K_A, D * D), D ** -0.5, 0.25)
    fine_upsample_bias = bell_draw(key_list[8], (D,), 0.3, 3.0)
    coarse_down = bell_draw(key_list[9], (K_B, D * D), (K_B * D) ** -0.5, 0.0625)
    coarse_down_bias = bell_draw(key_list[10], (D,), 0.3, 3.0)
    coarse_isometric = bell_draw(key_list[11], (ISO_B, D * D), (ISO_B * D) ** -0.5, 0.0625)
    coarse_isometric_bias = bell_draw(key_list[12], (D,), 0.3, 3.0)
    coarse_upsample = bell_draw(key_list[13], (K_B, D * D), D ** -0.5, 0.25)
    coarse_upsample_bias = bell_draw(key_list[14], (D,), 0.3, 3.0)
    branch_gain = jnp.clip(1.0 + 0.18 * jax.random.normal(key_list[15], (D,), jnp.float32), 0.099609375, 1.8984375).astype(jnp.bfloat16)
    branch_bias = bell_draw(key_list[16], (D,), 0.3, 3.0)
    merge_weight = bell_draw(key_list[17], (2, D * D), (2 * D) ** -0.5, 0.1875)
    merge_bias = bell_draw(key_list[18], (D,), 0.3, 3.0)
    first_gain = jnp.clip(1.0 + 0.18 * jax.random.normal(key_list[19], (D,), jnp.float32), 0.099609375, 1.8984375).astype(jnp.bfloat16)
    first_bias = bell_draw(key_list[20], (D,), 0.3, 3.0)
    expand_weight = bell_draw(key_list[21], (D, FF), D ** -0.5, 0.25)
    expand_bias = bell_draw(key_list[22], (FF,), 0.3, 3.0)
    reduce_weight = bell_draw(key_list[23], (FF, D), FF ** -0.5, 0.125)
    reduce_bias = bell_draw(key_list[24], (D,), 0.3, 3.0)
    final_gain = jnp.clip(1.0 + 0.18 * jax.random.normal(key_list[25], (D,), jnp.float32), 0.099609375, 1.8984375).astype(jnp.bfloat16)
    final_bias = bell_draw(key_list[26], (D,), 0.3, 3.0)
    return {"series": series, "horizon": horizon, "cotangent": cotangent, "fine_down": fine_down, "fine_down_bias": fine_down_bias, "fine_isometric": fine_isometric, "fine_isometric_bias": fine_isometric_bias, "fine_upsample": fine_upsample, "fine_upsample_bias": fine_upsample_bias, "coarse_down": coarse_down, "coarse_down_bias": coarse_down_bias, "coarse_isometric": coarse_isometric, "coarse_isometric_bias": coarse_isometric_bias, "coarse_upsample": coarse_upsample, "coarse_upsample_bias": coarse_upsample_bias, "branch_gain": branch_gain, "branch_bias": branch_bias, "merge_weight": merge_weight, "merge_bias": merge_bias, "first_gain": first_gain, "first_bias": first_bias, "expand_weight": expand_weight, "expand_bias": expand_bias, "reduce_weight": reduce_weight, "reduce_bias": reduce_bias, "final_gain": final_gain, "final_bias": final_bias}


EPSILON = 1e-05
HIGHEST = lax.Precision.HIGHEST
HORIZON_ENDS = (192, 288, 432, 816)

@jax.custom_vjp
def low(v):
    return lax.optimization_barrier(v.astype(jnp.bfloat16)).astype(jnp.float32)

@jax.custom_vjp
def low_back(v):
    return v

def low_keep(v):
    return (low(v), None)

def low_pass(kept, grad):
    return (grad,)

def back_keep(v):
    return (v, None)

def back_low(kept, grad):
    return (low(grad),)
low.defvjp(low_keep, low_pass)
low_back.defvjp(back_keep, back_low)

def moving_trend(values, window):
    half_width = (window - 1) // 2
    axis_time = values.ndim - 2
    steps_total = values.shape[axis_time]
    widths = [(0, 0)] * axis_time + [(half_width, half_width), (0, 0)]
    padded = jnp.pad(values, widths, mode='edge')
    running = lax.slice_in_dim(padded, 0, steps_total, axis=axis_time)
    for offset in range(1, window):
        running = running + lax.slice_in_dim(padded, offset, offset + steps_total, axis=axis_time)
    return running / window

def layer_norm(values, norm_gain, norm_shift):
    average = lax.optimization_barrier(jnp.mean(values, axis=-1, keepdims=True))
    centered = values - average
    variance = lax.optimization_barrier(jnp.mean(centered * centered, axis=-1, keepdims=True))
    return centered * lax.rsqrt(variance + EPSILON) * norm_gain + norm_shift

def gelu_exact(values):
    return jax.nn.gelu(values, approximate=False)

def valid_masks(horizon, length_total):
    valid_ends = jnp.zeros(horizon.shape, jnp.int32)
    for number, ending in enumerate(HORIZON_ENDS):
        valid_ends = valid_ends + jnp.where(horizon == number, length_total * ending, 0).astype(jnp.int32)
    positions = jnp.arange(length_total, dtype=jnp.int32) * 816
    return (positions[None, :] < valid_ends[:, None]).astype(jnp.float32)

def branch_forward(values, params, kernel, norm_gain, norm_shift):
    down_weight, down_bias, isometric_weight, isometric_bias, upsample_weight, upsample_bias = params
    length_total, channels = values.shape
    season = values - moving_trend(values, kernel + 1)
    step_count = length_total // kernel + 1
    half_kernel = kernel // 2
    patches = jnp.pad(low(season), ((half_kernel, half_kernel), (0, 0))).reshape(step_count, kernel * channels)
    down_out = jnp.tanh(low_back(jnp.dot(patches, down_weight.reshape(kernel * channels, channels), precision=HIGHEST) + down_bias))
    shifted = jnp.pad(low(down_out), ((step_count - 1, 0), (0, 0)))
    positions = jnp.arange(step_count, dtype=jnp.int32)
    unfolded = shifted[positions[:, None] + positions[None, :]].reshape(step_count, step_count * channels)
    iso_out = jnp.tanh(low_back(jnp.dot(unfolded, isometric_weight.reshape(step_count * channels, channels), precision=HIGHEST) + isometric_bias))
    joined = layer_norm(iso_out + down_out, norm_gain, norm_shift)
    upward = jnp.einsum('sa,jab->sjb', low(joined), upsample_weight.reshape(kernel, channels, channels), precision=HIGHEST)
    upward = upward.reshape(step_count * kernel, channels)[:length_total]
    up_out = jnp.tanh(low_back(upward + upsample_bias))
    return layer_norm(up_out + season, norm_gain, norm_shift)

def layer_forward(values, mask_rows, params):
    fine_down, fine_down_bias, fine_isometric, fine_isometric_bias, fine_upsample, fine_upsample_bias, coarse_down, coarse_down_bias, coarse_isometric, coarse_isometric_bias, coarse_upsample, coarse_upsample_bias, branch_gain, branch_bias, merge_weight, merge_bias, first_gain, first_bias, expand_weight, expand_bias, reduce_weight, reduce_bias, final_gain, final_bias = params
    channels = values.shape[-1]
    fine_out = branch_forward(values, (fine_down, fine_down_bias, fine_isometric, fine_isometric_bias, fine_upsample, fine_upsample_bias), K_A, branch_gain, branch_bias)
    coarse_out = branch_forward(values, (coarse_down, coarse_down_bias, coarse_isometric, coarse_isometric_bias, coarse_upsample, coarse_upsample_bias), K_B, branch_gain, branch_bias)
    branch_low = jnp.concatenate([low(fine_out), low(coarse_out)], axis=-1)
    merged = low_back(jnp.dot(branch_low, merge_weight.reshape(2 * channels, channels), precision=HIGHEST) + merge_bias)
    normed = layer_norm(merged, first_gain, first_bias)
    expanded = low_back(jnp.dot(low(normed), expand_weight, precision=HIGHEST) + expand_bias)
    activated = gelu_exact(expanded)
    reduced = low_back(jnp.dot(low(activated), reduce_weight, precision=HIGHEST) + reduce_bias)
    return layer_norm(merged + reduced, final_gain, final_bias) * mask_rows

def reference(series, horizon, cotangent, fine_down, fine_down_bias, fine_isometric, fine_isometric_bias, fine_upsample, fine_upsample_bias, coarse_down, coarse_down_bias, coarse_isometric, coarse_isometric_bias, coarse_upsample, coarse_upsample_bias, branch_gain, branch_bias, merge_weight, merge_bias, first_gain, first_bias, expand_weight, expand_bias, reduce_weight, reduce_bias, final_gain, final_bias):
    weights = tuple((weight.astype(jnp.float32) for weight in (fine_down, fine_down_bias, fine_isometric, fine_isometric_bias, fine_upsample, fine_upsample_bias, coarse_down, coarse_down_bias, coarse_isometric, coarse_isometric_bias, coarse_upsample, coarse_upsample_bias, branch_gain, branch_bias, merge_weight, merge_bias, first_gain, first_bias, expand_weight, expand_bias, reduce_weight, reduce_bias, final_gain, final_bias)))
    masks = valid_masks(horizon, LEN)

    def one_series(gradient_sums, inputs):
        row_series, row_mask, row_cotangent = inputs

        def forward(values, params):
            return layer_forward(values, row_mask[:, None], params)
        output_row, pullback = jax.vjp(forward, row_series.astype(jnp.float32), weights)
        input_gradient, weight_gradients = pullback(row_cotangent.astype(jnp.float32))
        gradient_sums = jax.tree.map(lambda earlier, later: earlier + later, gradient_sums, weight_gradients)
        return (gradient_sums, (output_row, input_gradient))
    initial = jax.tree.map(jnp.zeros_like, weights)
    gradient_sums, (result, series_gradient) = lax.scan(one_series, initial, (series, masks, cotangent))
    g_fine_down, g_fine_down_bias, g_fine_isometric, g_fine_isometric_bias, g_fine_upsample, g_fine_upsample_bias, g_coarse_down, g_coarse_down_bias, g_coarse_isometric, g_coarse_isometric_bias, g_coarse_upsample, g_coarse_upsample_bias, g_branch_gain, g_branch_bias, g_merge_weight, g_merge_bias, g_first_gain, g_first_bias, g_expand_weight, g_expand_bias, g_reduce_weight, g_reduce_bias, g_final_gain, g_final_bias = gradient_sums
    return (result, series_gradient, g_fine_down, g_fine_down_bias, g_fine_isometric, g_fine_isometric_bias, g_fine_upsample, g_fine_upsample_bias, g_coarse_down, g_coarse_down_bias, g_coarse_isometric, g_coarse_isometric_bias, g_coarse_upsample, g_coarse_upsample_bias, g_branch_gain, g_branch_bias, g_merge_weight, g_merge_bias, g_first_gain, g_first_bias, g_expand_weight, g_expand_bias, g_reduce_weight, g_reduce_bias, g_final_gain, g_final_bias)
```

```python
from functools import partial

import jax
import jax.numpy as jnp
from jax import lax
from jax.experimental import pallas as pl
from jax.experimental.pallas import tpu as pltpu
from jax.sharding import PartitionSpec as P

K_A = 12
K_B = 16


EPSILON = 1e-05
HORIZON_ENDS = (192, 288, 432, 816)
FLOAT = jnp.float32
BFLOAT = jnp.bfloat16


def product(operand, matrix):
    return jnp.dot(operand, matrix, preferred_element_type=FLOAT)


def product_back(gradient, matrix):
    return lax.dot_general(gradient, matrix, (((1,), (1,)), ((), ())), preferred_element_type=FLOAT)


def valid_masks(horizon, length_total):
    valid_ends = jnp.zeros(horizon.shape, jnp.int32)
    for number, ending in enumerate(HORIZON_ENDS):
        valid_ends = valid_ends + jnp.where(horizon == number, length_total * ending, 0).astype(
            jnp.int32
        )
    positions = lax.iota(jnp.int32, length_total) * 816
    return (positions[None, :] < valid_ends[:, None]).astype(FLOAT)


def _pad8(count):
    return -(-count // 8)


def _assemble(weight_ref, wide_ref, taps, slab):
    rows = min(8, taps - 8 * slab)

    def step(number, carry):
        for inner in range(4):
            pair = number * 4 + inner
            start = pl.multiple_of(pair * 1024, 1024)
            values = weight_ref[8 * slab : 8 * slab + rows, pl.ds(start, 1024)].astype(FLOAT)
            if rows < 8:
                values = jnp.concatenate([values, jnp.zeros((8 - rows, 1024), FLOAT)], axis=0)
            both = jnp.concatenate([values[:, :512], values[:, 512:]], axis=0)
            first = pl.multiple_of(pair * 16, 16)
            wide_ref[pl.ds(first, 16), :] = both.astype(BFLOAT)
        return carry

    lax.fori_loop(0, 16, step, 0)


def _statistics(values):
    average = jnp.mean(values, axis=-1, keepdims=True)
    centered = values - average
    variance = jnp.mean(centered * centered, axis=-1, keepdims=True)
    scale = lax.rsqrt(variance + EPSILON)
    return centered * scale, scale


def _norm_back(grad, normalized, scale, gain):
    weighted = grad * gain
    first = jnp.mean(weighted, axis=-1, keepdims=True)
    second = jnp.mean(weighted * normalized, axis=-1, keepdims=True)
    return scale * (weighted - first - normalized * second)


def _lanes(values):
    return [values[:, 128 * block : 128 * (block + 1)] for block in range(4)]


def forward_kernel(
    kernel,
    steps,
    bias,
    series_ref,
    params_ref,
    down_ref,
    iso_ref,
    up_ref,
    low_ref,
    up_out_ref,
    season_ref,
    down_out_ref,
    iso_out_ref,
    joined_ref,
    columns_ref,
    edge_ref,
    spread_ref,
    order_ref,
    wide_ref,
    rows_ref,
    taps_ref,
    sum_ref,
    raised_ref,
):
    length = series_ref.shape[0]
    half = kernel // 2
    window = kernel + 1
    tap_slabs = _pad8(kernel)
    iso_slabs = _pad8(steps)
    number = pl.program_id(0)
    block = lax.rem(number, 4)

    def rearranged(pieces, slabs):
        ordered = jnp.dot(
            jnp.concatenate(pieces, axis=0), order_ref[...], preferred_element_type=FLOAT
        )
        rows_ref[0 : slabs * 128, :] = ordered.astype(BFLOAT)

    def contract(weight_ref, taps, slabs):
        total = sum_ref[...]
        for slab in range(slabs):
            _assemble(weight_ref, wide_ref, taps, slab)
            first = pl.multiple_of((slab * 4 + block) * 32, 32)
            total = total + jnp.dot(
                rows_ref[pl.ds(first, 32), :], wide_ref[...], preferred_element_type=FLOAT
            )
        sum_ref[...] = total

    @pl.when(number == 0)
    def _():
        source = lax.broadcasted_iota(jnp.int32, (1024, 1024), 0)
        target = lax.broadcasted_iota(jnp.int32, (1024, 1024), 1)
        wanted = (source & 127) * 8 + (source >> 7)
        order_ref[...] = jnp.where(target == wanted, 1.0, 0.0).astype(BFLOAT)
        edge_ref[16 : 16 + length, :] = series_ref[...].astype(FLOAT)
        edge_ref[0:16, :] = jnp.broadcast_to(edge_ref[16:17, :], (16, 512))
        edge_ref[16 + length : 32 + length, :] = jnp.broadcast_to(
            edge_ref[15 + length : 16 + length, :], (16, 512)
        )
        spread_ref[...] = jnp.zeros_like(spread_ref)
        for lane in range(4):
            columns = slice(128 * lane, 128 * (lane + 1))
            running = edge_ref[16 - half : 16 - half + length, columns]
            for offset in range(1, window):
                first = 16 - half + offset
                running = running + edge_ref[first : first + length, columns]
            season = edge_ref[16 : 16 + length, columns] - running / window
            season_ref[:, columns] = season
            spread_ref[lane, half : half + length, :] = season
        pieces = []
        for slab in range(tap_slabs):
            for lane in range(4):
                parts = []
                for tap in range(8 * slab, 8 * slab + 8):
                    if tap < kernel:
                        part = spread_ref[lane, pl.ds(tap, 32, stride=kernel), :]
                    else:
                        part = jnp.zeros((32, 128), FLOAT)
                    parts.append(part.astype(BFLOAT))
                pieces.append(jnp.concatenate(parts, axis=1))
        rearranged(pieces, tap_slabs)
        sum_ref[...] = jnp.zeros_like(sum_ref)
        for group in range(kernel // 4):
            for lane in range(4):
                stacked = jnp.concatenate(
                    [
                        spread_ref[lane, pl.ds(4 * group + inner, 32, stride=kernel), :]
                        for inner in range(4)
                    ],
                    axis=0,
                )
                columns_ref[
                    128 * lane : 128 * (lane + 1), 128 * group : 128 * (group + 1)
                ] = stacked.T.astype(BFLOAT)

    @pl.when(number < 4)
    def _():
        contract(down_ref, kernel, tap_slabs)

    @pl.when(number == 3)
    def _():
        down_out = jnp.tanh(sum_ref[...] + params_ref[bias + 0 : bias + 1, :])
        down_out_ref[...] = down_out
        edge_ref[0:32, :] = jnp.zeros((32, 512), FLOAT)
        edge_ref[32:64, :] = down_out
        place = lax.broadcasted_iota(jnp.int32, (128, 128), 0)
        for lane, values in enumerate(_lanes(down_out)):
            padded = jnp.concatenate([values, jnp.zeros((96, 128), FLOAT)], axis=0)
            columns_ref[128 * lane : 128 * (lane + 1), 32 * kernel :] = jnp.where(
                place < steps, padded, 0.0
            ).T.astype(BFLOAT)
        pieces = []
        for slab in range(iso_slabs):
            for lane in range(4):
                columns = slice(128 * lane, 128 * (lane + 1))
                parts = []
                for tap in range(8 * slab, 8 * slab + 8):
                    if tap < steps:
                        first = 33 - steps + tap
                        part = edge_ref[first : first + 32, columns]
                    else:
                        part = jnp.zeros((32, 128), FLOAT)
                    parts.append(part.astype(BFLOAT))
                pieces.append(jnp.concatenate(parts, axis=1))
        rearranged(pieces, iso_slabs)
        sum_ref[...] = jnp.zeros_like(sum_ref)

    @pl.when((number >= 4) & (number < 8))
    def _():
        contract(iso_ref, steps, iso_slabs)

    @pl.when(number == 7)
    def _():
        iso_out = jnp.tanh(sum_ref[...] + params_ref[bias + 1 : bias + 2, :])
        iso_out_ref[...] = iso_out
        normalized, _ = _statistics(iso_out + down_out_ref[...])
        keep = lax.broadcasted_iota(jnp.int32, (32, 512), 0) < steps
        joined = jnp.where(
            keep, normalized * params_ref[6:7, :] + params_ref[7:8, :], 0.0
        ).astype(BFLOAT)
        joined_ref[...] = joined
        stacked = jnp.concatenate(_lanes(joined), axis=0)
        for tap in range(8):
            ordered = jnp.dot(
                stacked,
                order_ref[128 * tap : 128 * (tap + 1), :],
                preferred_element_type=FLOAT,
            ).astype(BFLOAT)
            for lane in range(4):
                first = lane * 256 + tap * 32
                taps_ref[first : first + 32, :] = ordered[32 * lane : 32 * (lane + 1), :]
        raised_ref[...] = jnp.zeros_like(raised_ref)

    @pl.when(number >= 8)
    def _():
        for slab in range(tap_slabs):
            _assemble(up_ref, wide_ref, kernel, slab)
            raised_ref[slab * 256 : (slab + 1) * 256, :] += jnp.dot(
                taps_ref[pl.ds(pl.multiple_of(block * 256, 256), 256), :],
                wide_ref[...],
                preferred_element_type=FLOAT,
            )

    @pl.when(number == 11)
    def _():
        for tap in range(kernel):
            for lane in range(4):
                spread_ref[lane, pl.ds(tap, 32, stride=kernel), :] = raised_ref[
                    32 * tap : 32 * (tap + 1), 128 * lane : 128 * (lane + 1)
                ]

        def finish(chunk, carry):
            rows = pl.ds(pl.multiple_of(chunk * 32, 32), 32)
            raised = jnp.concatenate([spread_ref[lane, rows, :] for lane in range(4)], axis=1)
            up_out = jnp.tanh(raised + params_ref[bias + 2 : bias + 3, :])
            up_out_ref[rows, :] = up_out
            normalized, _ = _statistics(up_out + season_ref[rows, :])
            low_ref[rows, :] = (
                normalized * params_ref[6:7, :] + params_ref[7:8, :]
            ).astype(BFLOAT)
            return carry

        lax.fori_loop(0, length // 32, finish, 0)


def _product(wide_ref, right_ref, slab):
    return lax.dot_general(
        wide_ref[...],
        right_ref[slab * 256 : (slab + 1) * 256, :],
        (((1,), (1,)), ((), ())),
        preferred_element_type=FLOAT,
    )


def _diagonal(wide, wide_out_ref):
    for part in range(2):
        wide_out_ref[part] = wide[:, 128 * part : 128 * (part + 1)]
    lane = lax.broadcasted_iota(jnp.int32, (128, 128), 1) >> 5
    halves = []
    for part in range(2):
        total = jnp.zeros((128, 128), FLOAT)
        for inner in range(4):
            tap = part * 4 + inner
            rows = wide_out_ref[part, pl.ds(tap, 128, stride=8), :]
            total = jnp.where(lane == inner, rows, total)
        halves.append(total)
    return halves


def _split(values):
    first = values.astype(BFLOAT).astype(FLOAT)
    second = (values - first).astype(BFLOAT).astype(FLOAT)
    return first, second, values - first - second


def outer_kernel(
    devices,
    kernels,
    grad_ref,
    up_fine_ref,
    season_fine_ref,
    joined_fine_ref,
    up_coarse_ref,
    season_coarse_ref,
    joined_coarse_ref,
    params_ref,
    vectors_ref,
    send_ref,
    right_fine_ref,
    right_coarse_ref,
    outer_fine_ref,
    outer_coarse_ref,
    spread_ref,
    sums_ref,
):
    length = grad_ref.shape[0]
    gain = params_ref[6:7, :]
    empty = jnp.zeros((1, 512), FLOAT)
    known = vectors_ref.shape[0]
    sums_ref[0:known, :] = vectors_ref[...]
    sums_ref[known + 2 : known + 4, :] = jnp.zeros((2, 512), FLOAT)
    branches = (
        (up_fine_ref, season_fine_ref, right_fine_ref, outer_fine_ref),
        (up_coarse_ref, season_coarse_ref, right_coarse_ref, outer_coarse_ref),
    )
    for branch, (up_ref, season_ref, right_ref, outer_ref) in enumerate(branches):
        kernel = kernels[branch]
        columns = slice(512 * branch, 512 * (branch + 1))
        spread_ref[...] = jnp.zeros_like(spread_ref)

        def outer(chunk, carry):
            gain_sum, shift_sum, bias_sum = carry
            rows = pl.ds(pl.multiple_of(chunk * 32, 32), 32)
            grad = grad_ref[rows, columns]
            up_out = up_ref[rows, :]
            normalized, scale = _statistics(up_out + season_ref[rows, :])
            back = _norm_back(grad, normalized, scale, gain)
            outer_ref[rows, :] = back
            raised = (back * (1.0 - up_out * up_out)).astype(BFLOAT).astype(FLOAT)
            for lane, values in enumerate(_lanes(raised)):
                spread_ref[lane, rows, :] = values
            return (
                gain_sum + jnp.sum(grad * normalized, axis=0, keepdims=True),
                shift_sum + jnp.sum(grad, axis=0, keepdims=True),
                bias_sum + jnp.sum(raised, axis=0, keepdims=True),
            )

        gain_sum, shift_sum, bias_sum = lax.fori_loop(
            0, length // 32, outer, (empty, empty, empty)
        )
        sums_ref[known + branch : known + branch + 1, :] = bias_sum
        sums_ref[known + 2 : known + 3, :] += gain_sum
        sums_ref[known + 3 : known + 4, :] += shift_sum
        for tap in range(8 * _pad8(kernel)):
            rows = slice(32 * tap, 32 * (tap + 1))
            if tap < kernel:
                right_ref[rows, :] = jnp.concatenate(
                    [spread_ref[lane, pl.ds(tap, 32, stride=kernel), :] for lane in range(4)],
                    axis=1,
                ).astype(BFLOAT)
            else:
                right_ref[rows, :] = jnp.zeros((32, 512), BFLOAT)
    place = lax.broadcasted_iota(jnp.int32, (32, 512), 0)
    for target in range(devices):
        first = 64 * target
        block = slice(first + 32, first + 64)
        branch = 0 if target < kernels[0] else 1
        tap = target - branch * kernels[0]
        if tap < kernels[branch]:
            rows = branches[branch][2][32 * tap : 32 * (tap + 1), :]
            if target < known + 4:
                rows = rows.astype(FLOAT)
                for inner, part in enumerate(_split(sums_ref[target : target + 1, :])):
                    rows = jnp.where(place == 29 + inner, part, rows)
                rows = rows.astype(BFLOAT)
            send_ref[block, :] = rows
            send_ref[first : first + 32, :] = (joined_fine_ref, joined_coarse_ref)[branch][...]
        else:
            send_ref[first : first + 64, :] = jnp.zeros((64, 512), BFLOAT)


def inner_kernel(
    steps,
    slabs,
    right_in_ref,
    down_out_ref,
    iso_out_ref,
    params_ref,
    up_ref,
    iso_ref,
    pack_ref,
    grad_down_ref,
    sums_ref,
    rows_ref,
    wide_ref,
    right_ref,
    wide_out_ref,
    turned_ref,
    shift_ref,
    inner_ref,
):
    iso_slabs = _pad8(steps)
    number = pl.program_id(0)
    block = lax.rem(number, 4)
    gain = params_ref[6:7, :]

    def contract(weight_ref, taps, count, operand_ref):
        total = None
        for slab in range(count):
            _assemble(weight_ref, wide_ref, taps, slab)
            term = _product(wide_ref, operand_ref, slab)
            total = term if total is None else total + term
        first, second = _diagonal(total, wide_out_ref)
        folded = first + second
        folded = folded + pltpu.roll(folded, 64, 1)
        folded = folded + pltpu.roll(folded, 32, 1)
        turned_ref[pl.ds(pl.multiple_of(block * 128, 128), 128), :] = folded

    def collected():
        return turned_ref[...].T[0:32, :]

    @pl.when(number < 4)
    def _():
        contract(up_ref, up_ref.shape[0], slabs, right_in_ref)

    @pl.when(number == 3)
    def _():
        grad = collected()
        iso_out = iso_out_ref[...]
        normalized, scale = _statistics(iso_out + down_out_ref[...])
        back = _norm_back(grad, normalized, scale, gain)
        inner_ref[...] = back
        sums_ref[0:1, :] = jnp.sum(grad * normalized, axis=0, keepdims=True)
        sums_ref[1:2, :] = jnp.sum(grad, axis=0, keepdims=True)
        low = (back * (1.0 - iso_out * iso_out)).astype(BFLOAT)
        rows_ref[0:32, :] = low.astype(FLOAT)
        shift_ref[...] = jnp.zeros_like(shift_ref)
        shift_ref[32:64, :] = low.astype(FLOAT)
        for tap in range(8 * iso_slabs):
            if tap < steps:
                first = 31 + steps - tap
                values = shift_ref[first : first + 32, :].astype(BFLOAT)
            else:
                values = jnp.zeros((32, 512), BFLOAT)
            right_ref[32 * tap : 32 * (tap + 1), :] = values

    @pl.when(number >= 4)
    def _():
        contract(iso_ref, steps, iso_slabs, right_ref)

    @pl.when(number == 7)
    def _():
        down_out = down_out_ref[...]
        keep = lax.broadcasted_iota(jnp.int32, (32, 512), 0) < steps
        grad = jnp.where(keep, inner_ref[...] + collected(), 0.0)
        low = (grad * (1.0 - down_out * down_out)).astype(BFLOAT)
        grad_down_ref[...] = low
        rows_ref[32:64, :] = jnp.zeros((32, 512), FLOAT)
        rows_ref[steps : steps + 32, :] = low.astype(FLOAT)
        for item in range(2):
            high, middle, _ = _split(sums_ref[item : item + 1, :])
            first = 2 * steps + 2 * item
            rows_ref[first : first + 1, :] = high
            rows_ref[first + 1 : first + 2, :] = middle
        pack_ref[...] = rows_ref[0 : pack_ref.shape[0], :].astype(BFLOAT)


def series_kernel(
    kernels,
    grad_fine_ref,
    grad_coarse_ref,
    outer_fine_ref,
    outer_coarse_ref,
    fine_ref,
    coarse_ref,
    series_ref,
    spread_ref,
    wide_ref,
    right_ref,
    wide_out_ref,
    turned_ref,
):
    length = series_ref.shape[0]
    number = pl.program_id(0)
    block = lax.rem(number, 4)
    branches = (
        (grad_fine_ref, outer_fine_ref, fine_ref),
        (grad_coarse_ref, outer_coarse_ref, coarse_ref),
    )
    for branch, (grad_ref, outer_ref, weight_ref) in enumerate(branches):
        kernel = kernels[branch]
        half = kernel // 2
        window = kernel + 1

        @pl.when(number == 4 * branch)
        def _(grad_ref=grad_ref):
            for tap in range(8):
                right_ref[32 * tap : 32 * (tap + 1), :] = grad_ref[...]

        @pl.when((number >= 4 * branch) & (number < 4 * branch + 4))
        def _(weight_ref=weight_ref, kernel=kernel):
            for slab in range(_pad8(kernel)):
                _assemble(weight_ref, wide_ref, kernel, slab)
                halves = _diagonal(_product(wide_ref, right_ref, 0), wide_out_ref)
                rows = pl.ds(pl.multiple_of(block * 128, 128), 128)
                for part in range(2):
                    turned_ref[2 * slab + part, rows, :] = halves[part]

        @pl.when(number == 4 * branch + 3)
        def _(outer_ref=outer_ref, kernel=kernel, half=half, window=window, branch=branch):
            spread_ref[...] = jnp.zeros_like(spread_ref)
            for tap in range(kernel):
                lane0 = 32 * (tap % 4)
                if tap % 4 == 0:
                    turned = turned_ref[tap // 4].T
                for lane in range(4):
                    spread_ref[lane, pl.ds(tap, 32, stride=kernel), :] = turned[
                        lane0 : lane0 + 32, 128 * lane : 128 * (lane + 1)
                    ]
            for lane in range(4):
                columns = slice(128 * lane, 128 * (lane + 1))
                season = outer_ref[:, columns] + spread_ref[lane, half : half + length, :]
                spread_ref[lane, 0:24, :] = jnp.zeros((24, 128), FLOAT)
                spread_ref[lane, 24 : 24 + length, :] = season
                spread_ref[lane, 24 + length : 48 + length, :] = jnp.zeros((24, 128), FLOAT)
                running = spread_ref[lane, 24 - half : 24 - half + length, :]
                for offset in range(1, window):
                    first = 24 - half + offset
                    running = running + spread_ref[lane, first : first + length, :]
                row = lax.broadcasted_iota(jnp.int32, (16, 128), 0)
                head = jnp.maximum(half + 1 - row, 0).astype(FLOAT)
                tail = jnp.maximum(row + half - 14, 0).astype(FLOAT)
                top = jnp.sum(season[0:16, :] * head, axis=0, keepdims=True)
                bottom = jnp.sum(season[length - 16 :, :] * tail, axis=0, keepdims=True)
                place = lax.broadcasted_iota(jnp.int32, (length, 128), 0)
                running = jnp.where(place == 0, top, running)
                running = jnp.where(place == length - 1, bottom, running)
                result = season - running / window
                if branch > 0:
                    result = result + series_ref[:, columns]
                series_ref[:, columns] = result


def _blocks(start):
    def index(number):
        return (0, jnp.clip(number - start, 0, 3))

    return index


def _whole(shape):
    return pl.BlockSpec(shape, lambda number: (0,) * len(shape))


def forward_branch(series, params, weights, kernel, steps, bias):
    down, iso, up = weights
    length = series.shape[0]
    width = 128 * 512
    shapes = [
        jax.ShapeDtypeStruct((length, 512), BFLOAT),
        jax.ShapeDtypeStruct((length, 512), FLOAT),
        jax.ShapeDtypeStruct((length, 512), FLOAT),
        jax.ShapeDtypeStruct((32, 512), FLOAT),
        jax.ShapeDtypeStruct((32, 512), FLOAT),
        jax.ShapeDtypeStruct((32, 512), BFLOAT),
        jax.ShapeDtypeStruct((512, 32 * kernel + 128), BFLOAT),
    ]
    return pl.pallas_call(
        partial(forward_kernel, kernel, steps, bias),
        grid=(12,),
        in_specs=[
            _whole((length, 512)),
            _whole(params.shape),
            pl.BlockSpec((kernel, width), _blocks(0)),
            pl.BlockSpec((steps, width), _blocks(4)),
            pl.BlockSpec((kernel, width), _blocks(8)),
        ],
        out_specs=[_whole(item.shape) for item in shapes],
        out_shape=shapes,
        scratch_shapes=[
            pltpu.VMEM((length + 32, 512), FLOAT),
            pltpu.VMEM((4, 512, 128), FLOAT),
            pltpu.VMEM((1024, 1024), BFLOAT),
            pltpu.VMEM((1024, 512), BFLOAT),
            pltpu.VMEM((512, 1024), BFLOAT),
            pltpu.VMEM((1024, 1024), BFLOAT),
            pltpu.VMEM((32, 512), FLOAT),
            pltpu.VMEM((512, 512), FLOAT),
        ],
        cost_estimate=_cost(90e6),
    )(series, params, down, iso, up)


def outer_grads(grad, fine_saved, coarse_saved, params, vectors, devices):
    length = grad.shape[0]
    kernels = (K_A, K_B)
    shapes = [
        jax.ShapeDtypeStruct((devices * 64, 512), BFLOAT),
        jax.ShapeDtypeStruct((256 * _pad8(K_A), 512), BFLOAT),
        jax.ShapeDtypeStruct((256 * _pad8(K_B), 512), BFLOAT),
        jax.ShapeDtypeStruct((length, 512), FLOAT),
        jax.ShapeDtypeStruct((length, 512), FLOAT),
    ]
    return pl.pallas_call(
        partial(outer_kernel, devices, kernels),
        out_shape=shapes,
        scratch_shapes=[pltpu.VMEM((4, 512, 128), FLOAT), pltpu.VMEM((16, 512), FLOAT)],
        cost_estimate=_cost(1e5),
    )(
        grad,
        fine_saved[1],
        fine_saved[2],
        fine_saved[5],
        coarse_saved[1],
        coarse_saved[2],
        coarse_saved[5],
        params,
        vectors,
    )


def _cost(read):
    return pl.CostEstimate(flops=0, bytes_accessed=int(read), transcendentals=0)


def inner_grads(right, saved, params, iso, up):
    kernel, steps = up.shape[0], iso.shape[0]
    width = 128 * 512
    shapes = [
        jax.ShapeDtypeStruct((8 * _pad8(2 * steps + 4), 512), BFLOAT),
        jax.ShapeDtypeStruct((32, 512), BFLOAT),
    ]
    return pl.pallas_call(
        partial(inner_kernel, steps, _pad8(kernel)),
        grid=(8,),
        in_specs=[
            _whole(right.shape),
            _whole((32, 512)),
            _whole((32, 512)),
            _whole(params.shape),
            pl.BlockSpec((kernel, width), _blocks(0)),
            pl.BlockSpec((steps, width), _blocks(4)),
        ],
        out_specs=[_whole(item.shape) for item in shapes],
        out_shape=shapes,
        scratch_shapes=[
            pltpu.VMEM((8, 512), FLOAT),
            pltpu.VMEM((64, 512), FLOAT),
            pltpu.VMEM((1024, 512), BFLOAT),
            pltpu.VMEM((1024, 512), BFLOAT),
            pltpu.VMEM((2, 1024, 128), FLOAT),
            pltpu.VMEM((512, 128), FLOAT),
            pltpu.VMEM((96, 512), FLOAT),
            pltpu.VMEM((32, 512), FLOAT),
        ],
        cost_estimate=_cost(80e6),
    )(right, saved[3], saved[4], params, up, iso)


def series_grads(grads, outers, weights):
    length = outers[0].shape[0]
    width = 128 * 512
    shape = jax.ShapeDtypeStruct((length, 512), FLOAT)
    return pl.pallas_call(
        partial(series_kernel, (K_A, K_B)),
        grid=(8,),
        in_specs=[
            _whole((32, 512)),
            _whole((32, 512)),
            _whole((length, 512)),
            _whole((length, 512)),
            pl.BlockSpec((K_A, width), _blocks(0)),
            pl.BlockSpec((K_B, width), _blocks(4)),
        ],
        out_specs=_whole((length, 512)),
        out_shape=shape,
        scratch_shapes=[
            pltpu.VMEM((4, 512, 128), FLOAT),
            pltpu.VMEM((1024, 512), BFLOAT),
            pltpu.VMEM((256, 512), BFLOAT),
            pltpu.VMEM((2, 1024, 128), FLOAT),
            pltpu.VMEM((4, 512, 128), FLOAT),
        ],
        cost_estimate=_cost(80e6),
    )(grads[0], grads[1], outers[0], outers[1], weights[0], weights[1])


def _left_product(left, right):
    return lax.dot_general(left, right, (((0,), (0,)), ((), ())), preferred_element_type=FLOAT)


def table_kernel(*refs):
    table_ref = refs[-1]
    table_ref[...] = jnp.zeros_like(table_ref)
    row = 0
    for ref in refs[:-1]:
        values = ref[...].astype(FLOAT)
        for start in range(0, values.shape[0], 512):
            table_ref[row, :] = values[start : start + 512]
            row += 1


def vector_table(vectors):
    rows = sum(item.shape[0] for item in vectors) // 512
    return pl.pallas_call(
        table_kernel,
        out_shape=jax.ShapeDtypeStruct((8 * _pad8(rows), 512), FLOAT),
        cost_estimate=_cost(1e6),
    )(*vectors)


def dense_kernel(
    devices,
    fine_ref,
    coarse_ref,
    merge_ref,
    expand_ref,
    reduce_ref,
    params_ref,
    mask_ref,
    cotangent_ref,
    result_ref,
    branches_ref,
    rows_ref,
    sums_ref,
    merged_ref,
    normed_ref,
    wide_ref,
    active_ref,
    slope_ref,
    residual_ref,
    low_ref,
):
    length = fine_ref.shape[0]
    hidden = expand_ref.shape[1]
    merge_bias, first_gain, first_bias = [
        params_ref[item : item + 1, :] for item in range(8, 11)
    ]
    reduce_bias, final_gain, final_bias = [
        params_ref[item : item + 1, :] for item in range(11, 14)
    ]
    empty = jnp.zeros((1, 512), FLOAT)

    def chunks(step, carry):
        def run(chunk, carry):
            return step(pl.ds(pl.multiple_of(chunk * 32, 32), 32), carry)

        return lax.fori_loop(0, length // 32, run, carry)

    def total(values):
        return jnp.sum(values, axis=0, keepdims=True)

    own = 512 // devices
    shard = hidden // devices
    firsts = scatter_rows(devices, 512, hidden)

    def place(values, start, size, offset):
        values = values.astype(BFLOAT)
        for item in range(512 // size):
            row = firsts[start // size + item] + offset
            rows_ref[row : row + size, :] = values[item * size : (item + 1) * size, :]

    merged_ref[...] = (
        product(fine_ref[...], merge_ref[0:512, :])
        + product(coarse_ref[...], merge_ref[512:1024, :])
        + merge_bias
    )

    def first(rows, carry):
        normalized, _ = _statistics(merged_ref[rows, :])
        normed_ref[rows, :] = (normalized * first_gain + first_bias).astype(BFLOAT)
        return carry

    chunks(first, 0)
    for start in range(0, hidden, 512):
        columns = slice(start, start + 512)
        wide_ref[...] = product(normed_ref[...], expand_ref[:, columns])
        number = 14 + start // 512
        bias = params_ref[number : number + 1, :]

        def gate(rows, carry):
            values = wide_ref[rows, :] + bias
            chance = 0.5 + 0.5 * lax.erf(values * 0.7071067811865476)
            active_ref[rows, columns] = (values * chance).astype(BFLOAT)
            density = jnp.exp(-0.5 * values * values) * 0.3989422804014327
            slope_ref[rows, columns] = chance + values * density
            return carry

        chunks(gate, 0)
    wide_ref[...] = product(active_ref[...], reduce_ref[...])

    def final(rows, carry):
        bias_sum, gain_sum, shift_sum = carry
        normalized, scale = _statistics(merged_ref[rows, :] + (wide_ref[rows, :] + reduce_bias))
        mask = mask_ref[rows, :]
        result_ref[rows, :] = (normalized * final_gain + final_bias) * mask
        grad = cotangent_ref[rows, :].astype(FLOAT) * mask
        back = _norm_back(grad, normalized, scale, final_gain)
        residual_ref[rows, :] = back
        low = back.astype(BFLOAT)
        low_ref[rows, :] = low
        return (
            bias_sum + total(low.astype(FLOAT)),
            gain_sum + total(grad * normalized),
            shift_sum + total(grad),
        )

    bias_sum, gain_sum, shift_sum = chunks(final, (empty, empty, empty))
    sums_ref[3:4, :] = bias_sum
    sums_ref[4:5, :] = gain_sum
    sums_ref[5:6, :] = shift_sum
    for start in range(0, hidden, 512):
        columns = slice(start, start + 512)
        place(_left_product(active_ref[:, columns], low_ref[...]), start, shard, 2 * own + shard)
        wide_ref[...] = product_back(low_ref[...], reduce_ref[columns, :])

        def gate_back(rows, carry):
            low = (wide_ref[rows, :] * slope_ref[rows, columns]).astype(BFLOAT)
            active_ref[rows, columns] = low
            return carry + total(low.astype(FLOAT))

        number = 6 + start // 512
        sums_ref[number : number + 1, :] = chunks(gate_back, empty)
        place(_left_product(active_ref[:, columns], normed_ref[...]), start, shard, 2 * own)
    wide_ref[...] = product_back(active_ref[...], expand_ref[...])

    def first_back(rows, carry):
        bias_sum, gain_sum, shift_sum = carry
        normalized, scale = _statistics(merged_ref[rows, :])
        grad = wide_ref[rows, :]
        back = _norm_back(grad, normalized, scale, first_gain)
        low = (residual_ref[rows, :] + back).astype(BFLOAT)
        low_ref[rows, :] = low
        return (
            bias_sum + total(low.astype(FLOAT)),
            gain_sum + total(grad * normalized),
            shift_sum + total(grad),
        )

    bias_sum, gain_sum, shift_sum = chunks(first_back, (empty, empty, empty))
    sums_ref[0:1, :] = bias_sum
    sums_ref[1:2, :] = gain_sum
    sums_ref[2:3, :] = shift_sum
    for branch, low_in_ref in enumerate((fine_ref, coarse_ref)):
        columns = slice(512 * branch, 512 * (branch + 1))
        place(_left_product(low_in_ref[...], low_ref[...]), 0, own, branch * own)
        branches_ref[:, columns] = product_back(low_ref[...], merge_ref[columns, :])


def dense_block(devices, fine, coarse, merge, expand, reduce, params, mask, cotangent):
    length, channels = fine.shape
    hidden = expand.shape[1]
    known = 6 + hidden // channels
    shapes = [
        jax.ShapeDtypeStruct((length, channels), FLOAT),
        jax.ShapeDtypeStruct((length, 2 * channels), FLOAT),
        jax.ShapeDtypeStruct((2 * channels + 2 * hidden, channels), BFLOAT),
        jax.ShapeDtypeStruct((known, channels), FLOAT),
    ]
    return pl.pallas_call(
        partial(dense_kernel, devices),
        out_shape=shapes,
        scratch_shapes=[
            pltpu.VMEM((length, channels), FLOAT),
            pltpu.VMEM((length, channels), BFLOAT),
            pltpu.VMEM((length, channels), FLOAT),
            pltpu.VMEM((length, hidden), BFLOAT),
            pltpu.VMEM((length, hidden), FLOAT),
            pltpu.VMEM((length, channels), FLOAT),
            pltpu.VMEM((length, channels), BFLOAT),
        ],
        cost_estimate=_cost(70e6),
    )(fine, coarse, merge, expand, reduce, params, mask, cotangent)


def scatter_groups(devices):
    near = 8
    far = devices // near
    inside = [[first * near + item for item in range(near)] for first in range(far)]
    across = [[first * near + item for first in range(far)] for item in range(near)]
    return (inside, across)


def scatter_rows(devices, channels, hidden):
    own = channels // devices
    count = 2 * own + 2 * (hidden // devices)
    far = devices // 8
    return [((item % 8) * far + item // 8) * count for item in range(devices)]


def feed_part(rows, own):
    inside, _ = scatter_groups(rows.shape[1] // own)
    return lax.psum_scatter(
        rows, "dp", scatter_dimension=0, axis_index_groups=inside, tiled=True
    )


def feed_sums(part, own, hidden):
    channels = part.shape[1]
    _, across = scatter_groups(channels // own)
    pieces = lax.all_to_all(
        part.reshape(len(across[0]), -1, channels), "dp", 0, 0, axis_index_groups=across
    )
    summed = jnp.sum(pieces.astype(FLOAT), axis=0)
    first = 2 * own
    second = first + hidden
    return (
        summed[:first].reshape(2, own * channels),
        summed[first:second].T,
        summed[second:],
    )


def idle_kernel(*refs):
    del refs


def after(values, other):
    anywhere = pl.BlockSpec(memory_space=pl.ANY)
    return pl.pallas_call(
        idle_kernel,
        out_shape=jax.ShapeDtypeStruct(values.shape, values.dtype),
        in_specs=[anywhere, anywhere],
        out_specs=anywhere,
        input_output_aliases={0: 0},
        cost_estimate=_cost(1e5),
    )(values, other)


def exchange(values):
    return lax.all_to_all(values, "dp", 0, 0, tiled=False)


def weight_kernel(kernel, steps, offset, first, ups, columns_ref, grads_ref, *refs):
    blocks_ref = refs[0] if ups else None
    refs = refs[1:] if ups else refs
    down_ref, iso_ref, sums_ref = refs[:3]
    up_refs = refs[3 : 3 + ups]
    left_ref, right_ref, turned_ref, spread_ref = refs[3 + ups :]
    devices, own = columns_ref.shape[:2]
    width = devices * 32
    lane = lax.broadcasted_iota(jnp.int32, (own, 128), 1) >> 5
    for group in range(devices // 4):
        lanes = slice(128 * group, 128 * (group + 1))
        for piece in range(kernel // 4 + 1):
            start = offset + 128 * piece
            parts = [
                columns_ref[4 * group + item, :, start : start + 128].astype(FLOAT)
                for item in range(4)
            ]
            for inner in range(4 if piece < kernel // 4 else 1):
                total = parts[inner]
                for item in range(4):
                    if item != inner:
                        moved = pltpu.roll(parts[item], (32 * (item - inner)) % 128, 1)
                        total = jnp.where(lane == item, moved, total)
                if piece < kernel // 4:
                    tap = 4 * piece + inner
                    left_ref[own * tap : own * (tap + 1), lanes] = total.astype(BFLOAT)
                else:
                    turned_ref[:, lanes] = total
    place = lax.broadcasted_iota(jnp.int32, (own, width), 1) & 31
    ones = jnp.where(place < steps, 1.0, 0.0).astype(BFLOAT)

    def load(which):
        start = first + which * steps
        for item in range(devices):
            values = grads_ref[item, start : start + steps, :].astype(FLOAT)
            values = jnp.concatenate([values, jnp.zeros((32 - steps, 512), FLOAT)], axis=0)
            right_ref[32 * item : 32 * (item + 1), :] = values.astype(BFLOAT)

    def rows_out(values, out_ref, taps):
        for block, item in enumerate(_lanes(values)):
            spread_ref[block, 0 : values.shape[0], :] = item
        for channel in range(own):
            for block in range(4):
                start = 512 * channel + 128 * block
                out_ref[:, start : start + 128] = spread_ref[
                    block, pl.ds(channel, taps, stride=own), :
                ]

    load(1)
    left_ref[own * kernel : own * (kernel + 1), :] = ones
    values = product(left_ref[0 : own * (kernel + 1), :], right_ref[...])
    sums_ref[0:1, :] = values[own * kernel : own * kernel + 1, :]
    rows_out(values, down_ref, kernel)
    load(0)
    values = turned_ref[...]
    for tap in range(steps):
        shift = steps - 1 - tap
        moved = pltpu.roll(values, shift, 1) if shift else values
        moved = jnp.where((place >= shift) & (place < steps), moved, 0.0)
        left_ref[own * tap : own * (tap + 1), :] = moved.astype(BFLOAT)
    left_ref[own * steps : own * (steps + 1), :] = ones
    values = product(left_ref[0 : own * (steps + 1), :], right_ref[...])
    sums_ref[1:2, :] = values[own * steps : own * steps + 1, :]
    rows_out(values, iso_ref, steps)
    taps_before = 0
    for up_ref in up_refs:
        taps = up_ref.shape[0]
        values = blocks_ref[taps_before : taps_before + taps, 0:own, :].astype(FLOAT)
        rows_out(values.reshape(taps * own, 512), up_ref, taps)
        taps_before += taps


def weight_grads(columns, grads, blocks, kernel, steps, offset, first):
    devices, own = columns.shape[:2]
    channels = grads.shape[2]
    taps_up = () if blocks is None else (K_A, K_B)
    if own % 16 or devices % 4:
        iso_rows = grads[:, first : first + steps]
        down_rows = grads[:, first + steps : first + 2 * steps]
        down, iso = branch_products(
            columns[:, :, offset : offset + 32 * kernel + 128], iso_rows, down_rows, kernel
        )
        sums = [jnp.sum(item, axis=(0, 1), dtype=FLOAT) for item in (down_rows, iso_rows)]
        ups = []
        taps_before = 0
        for taps in taps_up:
            part = blocks[taps_before : taps_before + taps, :own].astype(FLOAT)
            ups.append(part.reshape(taps, own * channels))
            taps_before += taps
        return (down, iso, jnp.stack(sums, axis=0), *ups)
    shapes = [
        jax.ShapeDtypeStruct((kernel, own * channels), FLOAT),
        jax.ShapeDtypeStruct((steps, own * channels), FLOAT),
        jax.ShapeDtypeStruct((2, channels), FLOAT),
    ] + [jax.ShapeDtypeStruct((taps, own * channels), FLOAT) for taps in taps_up]
    highest = own * (max(kernel, steps) + 1)
    return pl.pallas_call(
        partial(weight_kernel, kernel, steps, offset, first, len(taps_up)),
        out_shape=shapes,
        scratch_shapes=[
            pltpu.VMEM((highest, devices * 32), BFLOAT),
            pltpu.VMEM((devices * 32, channels), BFLOAT),
            pltpu.VMEM((own, devices * 32), FLOAT),
            pltpu.VMEM((4, highest, 128), FLOAT),
        ],
        cost_estimate=_cost(17e6),
    )(columns, grads, *(() if blocks is None else (blocks,)))


def branch_products(columns, grad_iso, grad_down, kernel):
    devices, own = columns.shape[:2]
    steps, channels = grad_iso.shape[1:]
    patches = columns[:, :, : 32 * kernel].reshape(devices, own, kernel, 32)[..., :steps]
    down = jnp.einsum("nats,nsb->tab", patches, grad_down, preferred_element_type=FLOAT)
    mine = columns[:, :, 32 * kernel : 32 * kernel + steps]
    shifted = jnp.pad(mine, ((0, 0), (0, 0), (steps - 1, 0)))
    taps = jnp.stack([shifted[:, :, j : j + steps] for j in range(steps)], axis=0)
    iso = jnp.einsum("jnas,nsb->jab", taps, grad_iso, preferred_element_type=FLOAT)
    return (down.reshape(kernel, own * channels), iso.reshape(steps, own * channels))


def body(
    series,
    horizon,
    cotangent,
    fine_down,
    fine_down_bias,
    fine_isometric,
    fine_isometric_bias,
    fine_upsample,
    fine_upsample_bias,
    coarse_down,
    coarse_down_bias,
    coarse_isometric,
    coarse_isometric_bias,
    coarse_upsample,
    coarse_upsample_bias,
    branch_gain,
    branch_bias,
    merge_weight,
    merge_bias,
    first_gain,
    first_bias,
    expand_weight,
    expand_bias,
    reduce_weight,
    reduce_bias,
    final_gain,
    final_bias,
):
    batch_count, length_total, channels = series.shape
    row_count = batch_count * length_total
    devices = lax.axis_size("dp")
    own = channels // devices
    mask_rows = valid_masks(horizon, length_total).reshape(row_count, 1)
    steps = (fine_isometric.shape[0], coarse_isometric.shape[0])
    table = vector_table(
        [
            fine_down_bias,
            fine_isometric_bias,
            fine_upsample_bias,
            coarse_down_bias,
            coarse_isometric_bias,
            coarse_upsample_bias,
            branch_gain,
            branch_bias,
            merge_bias,
            first_gain,
            first_bias,
            reduce_bias,
            final_gain,
            final_bias,
            expand_bias,
        ]
    )
    fine_weights = (fine_down, fine_isometric, fine_upsample)
    coarse_weights = (coarse_down, coarse_isometric, coarse_upsample)
    rows_in = series.reshape(row_count, channels)
    fine_saved = forward_branch(rows_in, table, fine_weights, K_A, steps[0], 0)
    coarse_saved = forward_branch(rows_in, table, coarse_weights, K_B, steps[1], 3)
    columns_fine = exchange(fine_saved[6].reshape(devices, own, -1))
    columns_coarse = exchange(coarse_saved[6].reshape(devices, own, -1))
    merge_matrix = merge_weight.reshape(2 * channels, channels)
    result, grad_branches, dense_rows, vectors = dense_block(
        devices,
        after(fine_saved[0], columns_fine),
        coarse_saved[0],
        merge_matrix,
        expand_weight,
        reduce_weight,
        table,
        mask_rows,
        cotangent.reshape(row_count, channels),
    )
    result = result.reshape(batch_count, length_total, channels)
    known = vectors.shape[0]
    send, right_fine, right_coarse, outer_fine, outer_coarse = outer_grads(
        after(grad_branches, columns_coarse), fine_saved, coarse_saved, table, vectors, devices
    )
    received = exchange(send.reshape(devices, 64, channels))
    part = feed_part(after(dense_rows, send), own)
    pack_fine, down_fine = inner_grads(
        right_fine, fine_saved, table, fine_isometric, fine_upsample
    )
    pack_coarse, down_coarse = inner_grads(
        right_coarse, coarse_saved, table, coarse_isometric, coarse_upsample
    )
    packs = jnp.concatenate([pack_fine, pack_coarse], axis=0)
    packs = after(packs, received)
    down_coarse = after(down_coarse, packs)
    grads = lax.all_gather(packs, "dp", axis=0, tiled=False)
    second = pack_fine.shape[0]
    tap_product = jnp.einsum(
        "nsa,nsb->ab", received[:, :32], received[:, 32:], preferred_element_type=FLOAT
    )
    vector_sum = jnp.sum(received[:, 61:64].astype(FLOAT), axis=(0, 1)).reshape(1, channels)
    high = lax.reduce_precision(vector_sum, 8, 7)
    pair = jnp.concatenate([high, vector_sum - high], axis=0).astype(BFLOAT)
    blocks = jnp.concatenate(
        [
            tap_product.astype(BFLOAT).reshape(devices, own, channels),
            jnp.broadcast_to(pair[None], (devices, 2, channels)),
        ],
        axis=1,
    )
    blocks = exchange(blocks)
    series_gradient = series_grads(
        (down_fine, down_coarse), (outer_fine, outer_coarse), (fine_down, coarse_down)
    )
    part = after(part, series_gradient)
    dense = feed_sums(part, own, expand_weight.shape[1] // devices)
    series_gradient = series_gradient.reshape(series.shape)
    fine_down_gradient, fine_isometric_gradient, fine_sums = weight_grads(
        columns_fine, grads, None, K_A, steps[0], 0, 0
    )
    (
        coarse_down_gradient,
        coarse_isometric_gradient,
        coarse_sums,
        fine_upsample_gradient,
        coarse_upsample_gradient,
    ) = weight_grads(columns_coarse, grads, blocks, K_B, steps[1], 0, second)
    fine_down_bias_gradient, fine_isometric_bias_gradient = fine_sums[0], fine_sums[1]
    coarse_down_bias_gradient, coarse_isometric_bias_gradient = coarse_sums[0], coarse_sums[1]
    inner_sums = jnp.sum(
        grads[:, 2 * steps[0] : 2 * steps[0] + 4].astype(FLOAT)
        + grads[:, second + 2 * steps[1] : second + 2 * steps[1] + 4].astype(FLOAT),
        axis=0,
    )
    inner_sums = jnp.sum(inner_sums.reshape(2, 2, channels), axis=1)
    totals = jnp.sum(blocks[: known + 4, own:].astype(FLOAT), axis=1)
    merge_bias_gradient = totals[0]
    first_gain_gradient = totals[1]
    first_bias_gradient = totals[2]
    reduce_bias_gradient = totals[3]
    final_gain_gradient = totals[4]
    final_bias_gradient = totals[5]
    expand_bias_gradient = totals[6:known].reshape(-1)
    fine_upsample_bias_gradient = totals[known]
    coarse_upsample_bias_gradient = totals[known + 1]
    branch_gain_gradient = totals[known + 2] + inner_sums[0]
    branch_bias_gradient = totals[known + 3] + inner_sums[1]
    merge_weight_gradient, expand_weight_gradient, reduce_weight_gradient = dense
    return (
        result,
        series_gradient,
        fine_down_gradient,
        fine_down_bias_gradient,
        fine_isometric_gradient,
        fine_isometric_bias_gradient,
        fine_upsample_gradient,
        fine_upsample_bias_gradient,
        coarse_down_gradient,
        coarse_down_bias_gradient,
        coarse_isometric_gradient,
        coarse_isometric_bias_gradient,
        coarse_upsample_gradient,
        coarse_upsample_bias_gradient,
        branch_gain_gradient,
        branch_bias_gradient,
        merge_weight_gradient,
        merge_bias_gradient,
        first_gain_gradient,
        first_bias_gradient,
        expand_weight_gradient,
        expand_bias_gradient,
        reduce_weight_gradient,
        reduce_bias_gradient,
        final_gain_gradient,
        final_bias_gradient,
    )


def solution(mesh):
    in_specs = (
        P("dp", None, None),
        P("dp"),
        P("dp", None, None),
        P(),
        P(),
        P(),
        P(),
        P(),
        P(),
        P(),
        P(),
        P(),
        P(),
        P(),
        P(),
        P(),
        P(),
        P(),
        P(),
        P(),
        P(),
        P(),
        P(),
        P(),
        P(),
        P(),
        P(),
    )
    out_specs = (
        P("dp", None, None),
        P("dp", None, None),
        P(None, "dp"),
        P(),
        P(None, "dp"),
        P(),
        P(None, "dp"),
        P(),
        P(None, "dp"),
        P(),
        P(None, "dp"),
        P(),
        P(None, "dp"),
        P(),
        P(),
        P(),
        P(None, "dp"),
        P(),
        P(),
        P(),
        P(None, "dp"),
        P(),
        P("dp", None),
        P(),
        P(),
        P(),
    )
    return jax.shard_map(body, mesh=mesh, in_specs=in_specs, out_specs=out_specs, check_vma=False)
```

```python
from functools import partial

import jax
import jax.numpy as jnp
from jax import lax
from jax.experimental import pallas as pl
from jax.experimental.pallas import tpu as pltpu
from jax.sharding import PartitionSpec as P

K_A = 12
K_B = 16


EPSILON = 1e-05
HORIZON_ENDS = (192, 288, 432, 816)
FLOAT = jnp.float32
BFLOAT = jnp.bfloat16


def product(operand, matrix):
    return jnp.dot(operand, matrix, preferred_element_type=FLOAT)


def product_back(gradient, matrix):
    return lax.dot_general(gradient, matrix, (((1,), (1,)), ((), ())), preferred_element_type=FLOAT)


def valid_masks(horizon, length_total):
    valid_ends = jnp.zeros(horizon.shape, jnp.int32)
    for number, ending in enumerate(HORIZON_ENDS):
        valid_ends = valid_ends + jnp.where(horizon == number, length_total * ending, 0).astype(
            jnp.int32
        )
    positions = lax.iota(jnp.int32, length_total) * 816
    return (positions[None, :] < valid_ends[:, None]).astype(FLOAT)


def _pad8(count):
    return -(-count // 8)


def _assemble(weight_ref, wide_ref, taps, slab):
    rows = min(8, taps - 8 * slab)

    def step(number, carry):
        for inner in range(8):
            pair = number * 8 + inner
            start = pl.multiple_of(pair * 1024, 1024)
            values = weight_ref[8 * slab : 8 * slab + rows, pl.ds(start, 1024)].astype(FLOAT)
            if rows < 8:
                values = jnp.concatenate([values, jnp.zeros((8 - rows, 1024), FLOAT)], axis=0)
            both = jnp.concatenate([values[:, :512], values[:, 512:]], axis=0)
            first = pl.multiple_of(pair * 16, 16)
            wide_ref[pl.ds(first, 16), :] = both.astype(BFLOAT)
        return carry

    lax.fori_loop(0, 8, step, 0)


def _statistics(values):
    average = jnp.mean(values, axis=-1, keepdims=True)
    centered = values - average
    variance = jnp.mean(centered * centered, axis=-1, keepdims=True)
    scale = lax.rsqrt(variance + EPSILON)
    return centered * scale, scale


def _norm_back(grad, normalized, scale, gain):
    weighted = grad * gain
    first = jnp.mean(weighted, axis=-1, keepdims=True)
    second = jnp.mean(weighted * normalized, axis=-1, keepdims=True)
    return scale * (weighted - first - normalized * second)


def _lanes(values):
    return [values[:, 128 * block : 128 * (block + 1)] for block in range(4)]


def forward_kernel(
    kernel,
    steps,
    bias,
    series_ref,
    params_ref,
    down_ref,
    iso_ref,
    up_ref,
    low_ref,
    up_out_ref,
    season_ref,
    down_out_ref,
    iso_out_ref,
    joined_ref,
    columns_ref,
    edge_ref,
    spread_ref,
    order_ref,
    wide_ref,
    rows_ref,
    taps_ref,
    sum_ref,
    raised_ref,
):
    length = series_ref.shape[0]
    half = kernel // 2
    window = kernel + 1
    tap_slabs = _pad8(kernel)
    iso_slabs = _pad8(steps)
    number = pl.program_id(0)
    block = lax.rem(number, 4)

    def rearranged(pieces, slabs):
        ordered = jnp.dot(
            jnp.concatenate(pieces, axis=0), order_ref[...], preferred_element_type=FLOAT
        )
        rows_ref[0 : slabs * 128, :] = ordered.astype(BFLOAT)

    def contract(weight_ref, taps, slabs):
        total = sum_ref[...]
        for slab in range(slabs):
            _assemble(weight_ref, wide_ref, taps, slab)
            first = pl.multiple_of((slab * 4 + block) * 32, 32)
            total = total + jnp.dot(
                rows_ref[pl.ds(first, 32), :], wide_ref[...], preferred_element_type=FLOAT
            )
        sum_ref[...] = total

    @pl.when(number == 0)
    def _():
        source = lax.broadcasted_iota(jnp.int32, (1024, 1024), 0)
        target = lax.broadcasted_iota(jnp.int32, (1024, 1024), 1)
        wanted = (source & 127) * 8 + (source >> 7)
        order_ref[...] = jnp.where(target == wanted, 1.0, 0.0).astype(BFLOAT)
        edge_ref[16 : 16 + length, :] = series_ref[...].astype(FLOAT)
        edge_ref[0:16, :] = jnp.broadcast_to(edge_ref[16:17, :], (16, 512))
        edge_ref[16 + length : 32 + length, :] = jnp.broadcast_to(
            edge_ref[15 + length : 16 + length, :], (16, 512)
        )
        spread_ref[...] = jnp.zeros_like(spread_ref)
        for lane in range(4):
            columns = slice(128 * lane, 128 * (lane + 1))
            running = edge_ref[16 - half : 16 - half + length, columns]
            for offset in range(1, window):
                first = 16 - half + offset
                running = running + edge_ref[first : first + length, columns]
            season = edge_ref[16 : 16 + length, columns] - running / window
            season_ref[:, columns] = season
            spread_ref[lane, half : half + length, :] = season
        pieces = []
        for slab in range(tap_slabs):
            for lane in range(4):
                parts = []
                for tap in range(8 * slab, 8 * slab + 8):
                    if tap < kernel:
                        part = spread_ref[lane, pl.ds(tap, 32, stride=kernel), :]
                    else:
                        part = jnp.zeros((32, 128), FLOAT)
                    parts.append(part.astype(BFLOAT))
                pieces.append(jnp.concatenate(parts, axis=1))
        rearranged(pieces, tap_slabs)
        sum_ref[...] = jnp.zeros_like(sum_ref)
        for group in range(kernel // 4):
            for lane in range(4):
                stacked = jnp.concatenate(
                    [
                        spread_ref[lane, pl.ds(4 * group + inner, 32, stride=kernel), :]
                        for inner in range(4)
                    ],
                    axis=0,
                )
                columns_ref[
                    128 * lane : 128 * (lane + 1), 128 * group : 128 * (group + 1)
                ] = stacked.T.astype(BFLOAT)

    @pl.when(number < 4)
    def _():
        contract(down_ref, kernel, tap_slabs)

    @pl.when(number == 3)
    def _():
        down_out = jnp.tanh(sum_ref[...] + params_ref[bias + 0 : bias + 1, :])
        down_out_ref[...] = down_out
        edge_ref[0:32, :] = jnp.zeros((32, 512), FLOAT)
        edge_ref[32:64, :] = down_out
        place = lax.broadcasted_iota(jnp.int32, (128, 128), 0)
        for lane, values in enumerate(_lanes(down_out)):
            padded = jnp.concatenate([values, jnp.zeros((96, 128), FLOAT)], axis=0)
            columns_ref[128 * lane : 128 * (lane + 1), 32 * kernel :] = jnp.where(
                place < steps, padded, 0.0
            ).T.astype(BFLOAT)
        pieces = []
        for slab in range(iso_slabs):
            for lane in range(4):
                columns = slice(128 * lane, 128 * (lane + 1))
                parts = []
                for tap in range(8 * slab, 8 * slab + 8):
                    if tap < steps:
                        first = 33 - steps + tap
                        part = edge_ref[first : first + 32, columns]
                    else:
                        part = jnp.zeros((32, 128), FLOAT)
                    parts.append(part.astype(BFLOAT))
                pieces.append(jnp.concatenate(parts, axis=1))
        rearranged(pieces, iso_slabs)
        sum_ref[...] = jnp.zeros_like(sum_ref)

    @pl.when((number >= 4) & (number < 8))
    def _():
        contract(iso_ref, steps, iso_slabs)

    @pl.when(number == 7)
    def _():
        iso_out = jnp.tanh(sum_ref[...] + params_ref[bias + 1 : bias + 2, :])
        iso_out_ref[...] = iso_out
        normalized, _ = _statistics(iso_out + down_out_ref[...])
        keep = lax.broadcasted_iota(jnp.int32, (32, 512), 0) < steps
        joined = jnp.where(
            keep, normalized * params_ref[6:7, :] + params_ref[7:8, :], 0.0
        ).astype(BFLOAT)
        joined_ref[...] = joined
        stacked = jnp.concatenate(_lanes(joined), axis=0)
        for tap in range(8):
            ordered = jnp.dot(
                stacked,
                order_ref[128 * tap : 128 * (tap + 1), :],
                preferred_element_type=FLOAT,
            ).astype(BFLOAT)
            for lane in range(4):
                first = lane * 256 + tap * 32
                taps_ref[first : first + 32, :] = ordered[32 * lane : 32 * (lane + 1), :]
        raised_ref[...] = jnp.zeros_like(raised_ref)

    @pl.when(number >= 8)
    def _():
        for slab in range(tap_slabs):
            _assemble(up_ref, wide_ref, kernel, slab)
            raised_ref[slab * 256 : (slab + 1) * 256, :] += jnp.dot(
                taps_ref[pl.ds(pl.multiple_of(block * 256, 256), 256), :],
                wide_ref[...],
                preferred_element_type=FLOAT,
            )

    @pl.when(number == 11)
    def _():
        for tap in range(kernel):
            for lane in range(4):
                spread_ref[lane, pl.ds(tap, 32, stride=kernel), :] = raised_ref[
                    32 * tap : 32 * (tap + 1), 128 * lane : 128 * (lane + 1)
                ]

        def finish(chunk, carry):
            rows = pl.ds(pl.multiple_of(chunk * 32, 32), 32)
            raised = jnp.concatenate([spread_ref[lane, rows, :] for lane in range(4)], axis=1)
            up_out = jnp.tanh(raised + params_ref[bias + 2 : bias + 3, :])
            up_out_ref[rows, :] = up_out
            normalized, _ = _statistics(up_out + season_ref[rows, :])
            low_ref[rows, :] = (
                normalized * params_ref[6:7, :] + params_ref[7:8, :]
            ).astype(BFLOAT)
            return carry

        lax.fori_loop(0, length // 32, finish, 0)


def _product(wide_ref, right_ref, slab):
    return lax.dot_general(
        wide_ref[...],
        right_ref[slab * 256 : (slab + 1) * 256, :],
        (((1,), (1,)), ((), ())),
        preferred_element_type=FLOAT,
    )


def _diagonal(wide, wide_out_ref):
    for part in range(2):
        wide_out_ref[part] = wide[:, 128 * part : 128 * (part + 1)]
    lane = lax.broadcasted_iota(jnp.int32, (128, 128), 1) >> 5
    halves = []
    for part in range(2):
        total = jnp.zeros((128, 128), FLOAT)
        for inner in range(4):
            tap = part * 4 + inner
            rows = wide_out_ref[part, pl.ds(tap, 128, stride=8), :]
            total = jnp.where(lane == inner, rows, total)
        halves.append(total)
    return halves


def _split(values):
    first = values.astype(BFLOAT).astype(FLOAT)
    second = (values - first).astype(BFLOAT).astype(FLOAT)
    return first, second, values - first - second


def outer_kernel(
    devices,
    kernels,
    grad_ref,
    up_fine_ref,
    season_fine_ref,
    joined_fine_ref,
    up_coarse_ref,
    season_coarse_ref,
    joined_coarse_ref,
    params_ref,
    vectors_ref,
    send_ref,
    right_fine_ref,
    right_coarse_ref,
    outer_fine_ref,
    outer_coarse_ref,
    spread_ref,
    sums_ref,
):
    length = grad_ref.shape[0]
    gain = params_ref[6:7, :]
    empty = jnp.zeros((1, 512), FLOAT)
    known = vectors_ref.shape[0]
    sums_ref[0:known, :] = vectors_ref[...]
    sums_ref[known + 2 : known + 4, :] = jnp.zeros((2, 512), FLOAT)
    branches = (
        (up_fine_ref, season_fine_ref, right_fine_ref, outer_fine_ref),
        (up_coarse_ref, season_coarse_ref, right_coarse_ref, outer_coarse_ref),
    )
    for branch, (up_ref, season_ref, right_ref, outer_ref) in enumerate(branches):
        kernel = kernels[branch]
        columns = slice(512 * branch, 512 * (branch + 1))
        spread_ref[...] = jnp.zeros_like(spread_ref)

        def outer(chunk, carry):
            gain_sum, shift_sum, bias_sum = carry
            rows = pl.ds(pl.multiple_of(chunk * 32, 32), 32)
            grad = grad_ref[rows, columns]
            up_out = up_ref[rows, :]
            normalized, scale = _statistics(up_out + season_ref[rows, :])
            back = _norm_back(grad, normalized, scale, gain)
            outer_ref[rows, :] = back
            raised = (back * (1.0 - up_out * up_out)).astype(BFLOAT).astype(FLOAT)
            for lane, values in enumerate(_lanes(raised)):
                spread_ref[lane, rows, :] = values
            return (
                gain_sum + jnp.sum(grad * normalized, axis=0, keepdims=True),
                shift_sum + jnp.sum(grad, axis=0, keepdims=True),
                bias_sum + jnp.sum(raised, axis=0, keepdims=True),
            )

        gain_sum, shift_sum, bias_sum = lax.fori_loop(
            0, length // 32, outer, (empty, empty, empty)
        )
        sums_ref[known + branch : known + branch + 1, :] = bias_sum
        sums_ref[known + 2 : known + 3, :] += gain_sum
        sums_ref[known + 3 : known + 4, :] += shift_sum
        for tap in range(8 * _pad8(kernel)):
            rows = slice(32 * tap, 32 * (tap + 1))
            if tap < kernel:
                right_ref[rows, :] = jnp.concatenate(
                    [spread_ref[lane, pl.ds(tap, 32, stride=kernel), :] for lane in range(4)],
                    axis=1,
                ).astype(BFLOAT)
            else:
                right_ref[rows, :] = jnp.zeros((32, 512), BFLOAT)
    place = lax.broadcasted_iota(jnp.int32, (32, 512), 0)
    for target in range(devices):
        first = 64 * target
        block = slice(first + 32, first + 64)
        branch = 0 if target < kernels[0] else 1
        tap = target - branch * kernels[0]
        if tap < kernels[branch]:
            rows = branches[branch][2][32 * tap : 32 * (tap + 1), :]
            if target < known + 4:
                rows = rows.astype(FLOAT)
                for inner, part in enumerate(_split(sums_ref[target : target + 1, :])):
                    rows = jnp.where(place == 29 + inner, part, rows)
                rows = rows.astype(BFLOAT)
            send_ref[block, :] = rows
            send_ref[first : first + 32, :] = (joined_fine_ref, joined_coarse_ref)[branch][...]
        else:
            send_ref[first : first + 64, :] = jnp.zeros((64, 512), BFLOAT)


def inner_kernel(
    steps,
    slabs,
    right_in_ref,
    down_out_ref,
    iso_out_ref,
    params_ref,
    up_ref,
    iso_ref,
    pack_ref,
    grad_down_ref,
    sums_ref,
    rows_ref,
    wide_ref,
    right_ref,
    wide_out_ref,
    turned_ref,
    shift_ref,
    inner_ref,
):
    iso_slabs = _pad8(steps)
    number = pl.program_id(0)
    block = lax.rem(number, 4)
    gain = params_ref[6:7, :]

    def contract(weight_ref, taps, count, operand_ref):
        total = None
        for slab in range(count):
            _assemble(weight_ref, wide_ref, taps, slab)
            term = _product(wide_ref, operand_ref, slab)
            total = term if total is None else total + term
        first, second = _diagonal(total, wide_out_ref)
        folded = first + second
        folded = folded + pltpu.roll(folded, 64, 1)
        folded = folded + pltpu.roll(folded, 32, 1)
        turned_ref[pl.ds(pl.multiple_of(block * 128, 128), 128), :] = folded

    def collected():
        return turned_ref[...].T[0:32, :]

    @pl.when(number < 4)
    def _():
        contract(up_ref, up_ref.shape[0], slabs, right_in_ref)

    @pl.when(number == 3)
    def _():
        grad = collected()
        iso_out = iso_out_ref[...]
        normalized, scale = _statistics(iso_out + down_out_ref[...])
        back = _norm_back(grad, normalized, scale, gain)
        inner_ref[...] = back
        sums_ref[0:1, :] = jnp.sum(grad * normalized, axis=0, keepdims=True)
        sums_ref[1:2, :] = jnp.sum(grad, axis=0, keepdims=True)
        low = (back * (1.0 - iso_out * iso_out)).astype(BFLOAT)
        rows_ref[0:32, :] = low.astype(FLOAT)
        shift_ref[...] = jnp.zeros_like(shift_ref)
        shift_ref[32:64, :] = low.astype(FLOAT)
        for tap in range(8 * iso_slabs):
            if tap < steps:
                first = 31 + steps - tap
                values = shift_ref[first : first + 32, :].astype(BFLOAT)
            else:
                values = jnp.zeros((32, 512), BFLOAT)
            right_ref[32 * tap : 32 * (tap + 1), :] = values

    @pl.when(number >= 4)
    def _():
        contract(iso_ref, steps, iso_slabs, right_ref)

    @pl.when(number == 7)
    def _():
        down_out = down_out_ref[...]
        keep = lax.broadcasted_iota(jnp.int32, (32, 512), 0) < steps
        grad = jnp.where(keep, inner_ref[...] + collected(), 0.0)
        low = (grad * (1.0 - down_out * down_out)).astype(BFLOAT)
        grad_down_ref[...] = low
        rows_ref[32:64, :] = jnp.zeros((32, 512), FLOAT)
        rows_ref[steps : steps + 32, :] = low.astype(FLOAT)
        for item in range(2):
            high, middle, _ = _split(sums_ref[item : item + 1, :])
            first = 2 * steps + 2 * item
            rows_ref[first : first + 1, :] = high
            rows_ref[first + 1 : first + 2, :] = middle
        pack_ref[...] = rows_ref[0 : pack_ref.shape[0], :].astype(BFLOAT)


def series_kernel(
    kernels,
    grad_fine_ref,
    grad_coarse_ref,
    outer_fine_ref,
    outer_coarse_ref,
    fine_ref,
    coarse_ref,
    series_ref,
    spread_ref,
    wide_ref,
    right_ref,
    wide_out_ref,
    turned_ref,
):
    length = series_ref.shape[0]
    number = pl.program_id(0)
    block = lax.rem(number, 4)
    branches = (
        (grad_fine_ref, outer_fine_ref, fine_ref),
        (grad_coarse_ref, outer_coarse_ref, coarse_ref),
    )
    for branch, (grad_ref, outer_ref, weight_ref) in enumerate(branches):
        kernel = kernels[branch]
        half = kernel // 2
        window = kernel + 1

        @pl.when(number == 4 * branch)
        def _(grad_ref=grad_ref):
            for tap in range(8):
                right_ref[32 * tap : 32 * (tap + 1), :] = grad_ref[...]

        @pl.when((number >= 4 * branch) & (number < 4 * branch + 4))
        def _(weight_ref=weight_ref, kernel=kernel):
            for slab in range(_pad8(kernel)):
                _assemble(weight_ref, wide_ref, kernel, slab)
                halves = _diagonal(_product(wide_ref, right_ref, 0), wide_out_ref)
                rows = pl.ds(pl.multiple_of(block * 128, 128), 128)
                for part in range(2):
                    turned_ref[2 * slab + part, rows, :] = halves[part]

        @pl.when(number == 4 * branch + 3)
        def _(outer_ref=outer_ref, kernel=kernel, half=half, window=window, branch=branch):
            spread_ref[...] = jnp.zeros_like(spread_ref)
            for tap in range(kernel):
                lane0 = 32 * (tap % 4)
                if tap % 4 == 0:
                    turned = turned_ref[tap // 4].T
                for lane in range(4):
                    spread_ref[lane, pl.ds(tap, 32, stride=kernel), :] = turned[
                        lane0 : lane0 + 32, 128 * lane : 128 * (lane + 1)
                    ]
            for lane in range(4):
                columns = slice(128 * lane, 128 * (lane + 1))
                season = outer_ref[:, columns] + spread_ref[lane, half : half + length, :]
                spread_ref[lane, 0:24, :] = jnp.zeros((24, 128), FLOAT)
                spread_ref[lane, 24 : 24 + length, :] = season
                spread_ref[lane, 24 + length : 48 + length, :] = jnp.zeros((24, 128), FLOAT)
                running = spread_ref[lane, 24 - half : 24 - half + length, :]
                for offset in range(1, window):
                    first = 24 - half + offset
                    running = running + spread_ref[lane, first : first + length, :]
                row = lax.broadcasted_iota(jnp.int32, (16, 128), 0)
                head = jnp.maximum(half + 1 - row, 0).astype(FLOAT)
                tail = jnp.maximum(row + half - 14, 0).astype(FLOAT)
                top = jnp.sum(season[0:16, :] * head, axis=0, keepdims=True)
                bottom = jnp.sum(season[length - 16 :, :] * tail, axis=0, keepdims=True)
                place = lax.broadcasted_iota(jnp.int32, (length, 128), 0)
                running = jnp.where(place == 0, top, running)
                running = jnp.where(place == length - 1, bottom, running)
                result = season - running / window
                if branch > 0:
                    result = result + series_ref[:, columns]
                series_ref[:, columns] = result


def _blocks(start):
    def index(number):
        return (0, jnp.clip(number - start, 0, 3))

    return index


def _whole(shape):
    return pl.BlockSpec(shape, lambda number: (0,) * len(shape))


def forward_branch(series, params, weights, kernel, steps, bias):
    down, iso, up = weights
    length = series.shape[0]
    width = 128 * 512
    shapes = [
        jax.ShapeDtypeStruct((length, 512), BFLOAT),
        jax.ShapeDtypeStruct((length, 512), FLOAT),
        jax.ShapeDtypeStruct((length, 512), FLOAT),
        jax.ShapeDtypeStruct((32, 512), FLOAT),
        jax.ShapeDtypeStruct((32, 512), FLOAT),
        jax.ShapeDtypeStruct((32, 512), BFLOAT),
        jax.ShapeDtypeStruct((512, 32 * kernel + 128), BFLOAT),
    ]
    return pl.pallas_call(
        partial(forward_kernel, kernel, steps, bias),
        grid=(12,),
        in_specs=[
            _whole((length, 512)),
            _whole(params.shape),
            pl.BlockSpec((kernel, width), _blocks(0)),
            pl.BlockSpec((steps, width), _blocks(4)),
            pl.BlockSpec((kernel, width), _blocks(8)),
        ],
        out_specs=[_whole(item.shape) for item in shapes],
        out_shape=shapes,
        scratch_shapes=[
            pltpu.VMEM((length + 32, 512), FLOAT),
            pltpu.VMEM((4, 512, 128), FLOAT),
            pltpu.VMEM((1024, 1024), BFLOAT),
            pltpu.VMEM((1024, 512), BFLOAT),
            pltpu.VMEM((512, 1024), BFLOAT),
            pltpu.VMEM((1024, 1024), BFLOAT),
            pltpu.VMEM((32, 512), FLOAT),
            pltpu.VMEM((512, 512), FLOAT),
        ],
        cost_estimate=_cost(90e6),
    )(series, params, down, iso, up)


def outer_grads(grad, fine_saved, coarse_saved, params, vectors, devices):
    length = grad.shape[0]
    kernels = (K_A, K_B)
    shapes = [
        jax.ShapeDtypeStruct((devices * 64, 512), BFLOAT),
        jax.ShapeDtypeStruct((256 * _pad8(K_A), 512), BFLOAT),
        jax.ShapeDtypeStruct((256 * _pad8(K_B), 512), BFLOAT),
        jax.ShapeDtypeStruct((length, 512), FLOAT),
        jax.ShapeDtypeStruct((length, 512), FLOAT),
    ]
    return pl.pallas_call(
        partial(outer_kernel, devices, kernels),
        out_shape=shapes,
        scratch_shapes=[pltpu.VMEM((4, 512, 128), FLOAT), pltpu.VMEM((16, 512), FLOAT)],
        cost_estimate=_cost(1e5),
    )(
        grad,
        fine_saved[1],
        fine_saved[2],
        fine_saved[5],
        coarse_saved[1],
        coarse_saved[2],
        coarse_saved[5],
        params,
        vectors,
    )


def _cost(read):
    return pl.CostEstimate(flops=0, bytes_accessed=int(read), transcendentals=0)


def inner_grads(right, saved, params, iso, up):
    kernel, steps = up.shape[0], iso.shape[0]
    width = 128 * 512
    shapes = [
        jax.ShapeDtypeStruct((8 * _pad8(2 * steps + 4), 512), BFLOAT),
        jax.ShapeDtypeStruct((32, 512), BFLOAT),
    ]
    return pl.pallas_call(
        partial(inner_kernel, steps, _pad8(kernel)),
        grid=(8,),
        in_specs=[
            _whole(right.shape),
            _whole((32, 512)),
            _whole((32, 512)),
            _whole(params.shape),
            pl.BlockSpec((kernel, width), _blocks(0)),
            pl.BlockSpec((steps, width), _blocks(4)),
        ],
        out_specs=[_whole(item.shape) for item in shapes],
        out_shape=shapes,
        scratch_shapes=[
            pltpu.VMEM((8, 512), FLOAT),
            pltpu.VMEM((64, 512), FLOAT),
            pltpu.VMEM((1024, 512), BFLOAT),
            pltpu.VMEM((1024, 512), BFLOAT),
            pltpu.VMEM((2, 1024, 128), FLOAT),
            pltpu.VMEM((512, 128), FLOAT),
            pltpu.VMEM((96, 512), FLOAT),
            pltpu.VMEM((32, 512), FLOAT),
        ],
        cost_estimate=_cost(80e6),
    )(right, saved[3], saved[4], params, up, iso)


def series_grads(grads, outers, weights):
    length = outers[0].shape[0]
    width = 128 * 512
    shape = jax.ShapeDtypeStruct((length, 512), FLOAT)
    return pl.pallas_call(
        partial(series_kernel, (K_A, K_B)),
        grid=(8,),
        in_specs=[
            _whole((32, 512)),
            _whole((32, 512)),
            _whole((length, 512)),
            _whole((length, 512)),
            pl.BlockSpec((K_A, width), _blocks(0)),
            pl.BlockSpec((K_B, width), _blocks(4)),
        ],
        out_specs=_whole((length, 512)),
        out_shape=shape,
        scratch_shapes=[
            pltpu.VMEM((4, 512, 128), FLOAT),
            pltpu.VMEM((1024, 512), BFLOAT),
            pltpu.VMEM((256, 512), BFLOAT),
            pltpu.VMEM((2, 1024, 128), FLOAT),
            pltpu.VMEM((4, 512, 128), FLOAT),
        ],
        cost_estimate=_cost(80e6),
    )(grads[0], grads[1], outers[0], outers[1], weights[0], weights[1])


def _left_product(left, right):
    return lax.dot_general(left, right, (((0,), (0,)), ((), ())), preferred_element_type=FLOAT)


def table_kernel(*refs):
    table_ref = refs[-1]
    table_ref[...] = jnp.zeros_like(table_ref)
    row = 0
    for ref in refs[:-1]:
        values = ref[...].astype(FLOAT)
        for start in range(0, values.shape[0], 512):
            table_ref[row, :] = values[start : start + 512]
            row += 1


def vector_table(vectors):
    rows = sum(item.shape[0] for item in vectors) // 512
    return pl.pallas_call(
        table_kernel,
        out_shape=jax.ShapeDtypeStruct((8 * _pad8(rows), 512), FLOAT),
        cost_estimate=_cost(1e6),
    )(*vectors)


def dense_kernel(
    devices,
    fine_ref,
    coarse_ref,
    merge_ref,
    expand_ref,
    reduce_ref,
    params_ref,
    mask_ref,
    cotangent_ref,
    result_ref,
    branches_ref,
    rows_ref,
    sums_ref,
    merged_ref,
    normed_ref,
    wide_ref,
    active_ref,
    slope_ref,
    residual_ref,
    low_ref,
):
    length = fine_ref.shape[0]
    hidden = expand_ref.shape[1]
    merge_bias, first_gain, first_bias = [
        params_ref[item : item + 1, :] for item in range(8, 11)
    ]
    reduce_bias, final_gain, final_bias = [
        params_ref[item : item + 1, :] for item in range(11, 14)
    ]
    empty = jnp.zeros((1, 512), FLOAT)

    def chunks(step, carry):
        def run(chunk, carry):
            return step(pl.ds(pl.multiple_of(chunk * 32, 32), 32), carry)

        return lax.fori_loop(0, length // 32, run, carry)

    def total(values):
        return jnp.sum(values, axis=0, keepdims=True)

    own = 512 // devices
    shard = hidden // devices
    firsts = scatter_rows(devices, 512, hidden)

    def place(values, start, size, offset):
        values = values.astype(BFLOAT)
        for item in range(512 // size):
            row = firsts[start // size + item] + offset
            rows_ref[row : row + size, :] = values[item * size : (item + 1) * size, :]

    merged_ref[...] = (
        product(fine_ref[...], merge_ref[0:512, :])
        + product(coarse_ref[...], merge_ref[512:1024, :])
        + merge_bias
    )

    def first(rows, carry):
        normalized, _ = _statistics(merged_ref[rows, :])
        normed_ref[rows, :] = (normalized * first_gain + first_bias).astype(BFLOAT)
        return carry

    chunks(first, 0)
    for start in range(0, hidden, 512):
        columns = slice(start, start + 512)
        wide_ref[...] = product(normed_ref[...], expand_ref[:, columns])
        number = 14 + start // 512
        bias = params_ref[number : number + 1, :]

        def gate(rows, carry):
            values = wide_ref[rows, :] + bias
            chance = 0.5 + 0.5 * lax.erf(values * 0.7071067811865476)
            active_ref[rows, columns] = (values * chance).astype(BFLOAT)
            density = jnp.exp(-0.5 * values * values) * 0.3989422804014327
            slope_ref[rows, columns] = chance + values * density
            return carry

        chunks(gate, 0)
    wide_ref[...] = product(active_ref[...], reduce_ref[...])

    def final(rows, carry):
        bias_sum, gain_sum, shift_sum = carry
        normalized, scale = _statistics(merged_ref[rows, :] + (wide_ref[rows, :] + reduce_bias))
        mask = mask_ref[rows, :]
        result_ref[rows, :] = (normalized * final_gain + final_bias) * mask
        grad = cotangent_ref[rows, :].astype(FLOAT) * mask
        back = _norm_back(grad, normalized, scale, final_gain)
        residual_ref[rows, :] = back
        low = back.astype(BFLOAT)
        low_ref[rows, :] = low
        return (
            bias_sum + total(low.astype(FLOAT)),
            gain_sum + total(grad * normalized),
            shift_sum + total(grad),
        )

    bias_sum, gain_sum, shift_sum = chunks(final, (empty, empty, empty))
    sums_ref[3:4, :] = bias_sum
    sums_ref[4:5, :] = gain_sum
    sums_ref[5:6, :] = shift_sum
    for start in range(0, hidden, 512):
        columns = slice(start, start + 512)
        place(_left_product(active_ref[:, columns], low_ref[...]), start, shard, 2 * own + shard)
        wide_ref[...] = product_back(low_ref[...], reduce_ref[columns, :])

        def gate_back(rows, carry):
            low = (wide_ref[rows, :] * slope_ref[rows, columns]).astype(BFLOAT)
            active_ref[rows, columns] = low
            return carry + total(low.astype(FLOAT))

        number = 6 + start // 512
        sums_ref[number : number + 1, :] = chunks(gate_back, empty)
        place(_left_product(active_ref[:, columns], normed_ref[...]), start, shard, 2 * own)
    wide_ref[...] = product_back(active_ref[...], expand_ref[...])

    def first_back(rows, carry):
        bias_sum, gain_sum, shift_sum = carry
        normalized, scale = _statistics(merged_ref[rows, :])
        grad = wide_ref[rows, :]
        back = _norm_back(grad, normalized, scale, first_gain)
        low = (residual_ref[rows, :] + back).astype(BFLOAT)
        low_ref[rows, :] = low
        return (
            bias_sum + total(low.astype(FLOAT)),
            gain_sum + total(grad * normalized),
            shift_sum + total(grad),
        )

    bias_sum, gain_sum, shift_sum = chunks(first_back, (empty, empty, empty))
    sums_ref[0:1, :] = bias_sum
    sums_ref[1:2, :] = gain_sum
    sums_ref[2:3, :] = shift_sum
    for branch, low_in_ref in enumerate((fine_ref, coarse_ref)):
        columns = slice(512 * branch, 512 * (branch + 1))
        place(_left_product(low_in_ref[...], low_ref[...]), 0, own, branch * own)
        branches_ref[:, columns] = product_back(low_ref[...], merge_ref[columns, :])


def dense_block(devices, fine, coarse, merge, expand, reduce, params, mask, cotangent):
    length, channels = fine.shape
    hidden = expand.shape[1]
    known = 6 + hidden // channels
    shapes = [
        jax.ShapeDtypeStruct((length, channels), FLOAT),
        jax.ShapeDtypeStruct((length, 2 * channels), FLOAT),
        jax.ShapeDtypeStruct((2 * channels + 2 * hidden, channels), BFLOAT),
        jax.ShapeDtypeStruct((known, channels), FLOAT),
    ]
    return pl.pallas_call(
        partial(dense_kernel, devices),
        out_shape=shapes,
        scratch_shapes=[
            pltpu.VMEM((length, channels), FLOAT),
            pltpu.VMEM((length, channels), BFLOAT),
            pltpu.VMEM((length, channels), FLOAT),
            pltpu.VMEM((length, hidden), BFLOAT),
            pltpu.VMEM((length, hidden), FLOAT),
            pltpu.VMEM((length, channels), FLOAT),
            pltpu.VMEM((length, channels), BFLOAT),
        ],
        cost_estimate=_cost(70e6),
    )(fine, coarse, merge, expand, reduce, params, mask, cotangent)


def scatter_groups(devices):
    near = 8
    far = devices // near
    inside = [[first * near + item for item in range(near)] for first in range(far)]
    across = [[first * near + item for first in range(far)] for item in range(near)]
    return (inside, across)


def scatter_rows(devices, channels, hidden):
    own = channels // devices
    count = 2 * own + 2 * (hidden // devices)
    far = devices // 8
    return [((item % 8) * far + item // 8) * count for item in range(devices)]


def feed_part(rows, own):
    inside, _ = scatter_groups(rows.shape[1] // own)
    return lax.psum_scatter(
        rows, "dp", scatter_dimension=0, axis_index_groups=inside, tiled=True
    )


def feed_sums(part, own, hidden):
    channels = part.shape[1]
    _, across = scatter_groups(channels // own)
    pieces = lax.all_to_all(
        part.reshape(len(across[0]), -1, channels), "dp", 0, 0, axis_index_groups=across
    )
    summed = jnp.sum(pieces.astype(FLOAT), axis=0)
    first = 2 * own
    second = first + hidden
    return (
        summed[:first].reshape(2, own * channels),
        summed[first:second].T,
        summed[second:],
    )


def idle_kernel(*refs):
    del refs


def after(values, other):
    anywhere = pl.BlockSpec(memory_space=pl.ANY)
    return pl.pallas_call(
        idle_kernel,
        out_shape=jax.ShapeDtypeStruct(values.shape, values.dtype),
        in_specs=[anywhere, anywhere],
        out_specs=anywhere,
        input_output_aliases={0: 0},
        cost_estimate=_cost(1e5),
    )(values, other)


def exchange(values):
    return lax.all_to_all(values, "dp", 0, 0, tiled=False)


def weight_kernel(kernel, steps, offset, first, ups, columns_ref, grads_ref, *refs):
    blocks_ref = refs[0] if ups else None
    refs = refs[1:] if ups else refs
    down_ref, iso_ref, sums_ref = refs[:3]
    up_refs = refs[3 : 3 + ups]
    left_ref, right_ref, turned_ref, spread_ref = refs[3 + ups :]
    devices, own = columns_ref.shape[:2]
    width = devices * 32
    lane = lax.broadcasted_iota(jnp.int32, (own, 128), 1) >> 5
    for group in range(devices // 4):
        lanes = slice(128 * group, 128 * (group + 1))
        for piece in range(kernel // 4 + 1):
            start = offset + 128 * piece
            parts = [
                columns_ref[4 * group + item, :, start : start + 128].astype(FLOAT)
                for item in range(4)
            ]
            for inner in range(4 if piece < kernel // 4 else 1):
                total = parts[inner]
                for item in range(4):
                    if item != inner:
                        moved = pltpu.roll(parts[item], (32 * (item - inner)) % 128, 1)
                        total = jnp.where(lane == item, moved, total)
                if piece < kernel // 4:
                    tap = 4 * piece + inner
                    left_ref[own * tap : own * (tap + 1), lanes] = total.astype(BFLOAT)
                else:
                    turned_ref[:, lanes] = total
    place = lax.broadcasted_iota(jnp.int32, (own, width), 1) & 31
    ones = jnp.where(place < steps, 1.0, 0.0).astype(BFLOAT)

    def load(which):
        start = first + which * steps
        for item in range(devices):
            values = grads_ref[item, start : start + steps, :].astype(FLOAT)
            values = jnp.concatenate([values, jnp.zeros((32 - steps, 512), FLOAT)], axis=0)
            right_ref[32 * item : 32 * (item + 1), :] = values.astype(BFLOAT)

    def rows_out(values, out_ref, taps):
        for block, item in enumerate(_lanes(values)):
            spread_ref[block, 0 : values.shape[0], :] = item
        for channel in range(own):
            for block in range(4):
                start = 512 * channel + 128 * block
                out_ref[:, start : start + 128] = spread_ref[
                    block, pl.ds(channel, taps, stride=own), :
                ]

    load(1)
    left_ref[own * kernel : own * (kernel + 1), :] = ones
    values = product(left_ref[0 : own * (kernel + 1), :], right_ref[...])
    sums_ref[0:1, :] = values[own * kernel : own * kernel + 1, :]
    rows_out(values, down_ref, kernel)
    load(0)
    values = turned_ref[...]
    for tap in range(steps):
        shift = steps - 1 - tap
        moved = pltpu.roll(values, shift, 1) if shift else values
        moved = jnp.where((place >= shift) & (place < steps), moved, 0.0)
        left_ref[own * tap : own * (tap + 1), :] = moved.astype(BFLOAT)
    left_ref[own * steps : own * (steps + 1), :] = ones
    values = product(left_ref[0 : own * (steps + 1), :], right_ref[...])
    sums_ref[1:2, :] = values[own * steps : own * steps + 1, :]
    rows_out(values, iso_ref, steps)
    taps_before = 0
    for up_ref in up_refs:
        taps = up_ref.shape[0]
        values = blocks_ref[taps_before : taps_before + taps, 0:own, :].astype(FLOAT)
        rows_out(values.reshape(taps * own, 512), up_ref, taps)
        taps_before += taps


def weight_grads(columns, grads, blocks, kernel, steps, offset, first):
    devices, own = columns.shape[:2]
    channels = grads.shape[2]
    taps_up = () if blocks is None else (K_A, K_B)
    if own % 16 or devices % 4:
        iso_rows = grads[:, first : first + steps]
        down_rows = grads[:, first + steps : first + 2 * steps]
        down, iso = branch_products(
            columns[:, :, offset : offset + 32 * kernel + 128], iso_rows, down_rows, kernel
        )
        sums = [jnp.sum(item, axis=(0, 1), dtype=FLOAT) for item in (down_rows, iso_rows)]
        ups = []
        taps_before = 0
        for taps in taps_up:
            part = blocks[taps_before : taps_before + taps, :own].astype(FLOAT)
            ups.append(part.reshape(taps, own * channels))
            taps_before += taps
        return (down, iso, jnp.stack(sums, axis=0), *ups)
    shapes = [
        jax.ShapeDtypeStruct((kernel, own * channels), FLOAT),
        jax.ShapeDtypeStruct((steps, own * channels), FLOAT),
        jax.ShapeDtypeStruct((2, channels), FLOAT),
    ] + [jax.ShapeDtypeStruct((taps, own * channels), FLOAT) for taps in taps_up]
    highest = own * (max(kernel, steps) + 1)
    return pl.pallas_call(
        partial(weight_kernel, kernel, steps, offset, first, len(taps_up)),
        out_shape=shapes,
        scratch_shapes=[
            pltpu.VMEM((highest, devices * 32), BFLOAT),
            pltpu.VMEM((devices * 32, channels), BFLOAT),
            pltpu.VMEM((own, devices * 32), FLOAT),
            pltpu.VMEM((4, highest, 128), FLOAT),
        ],
        cost_estimate=_cost(17e6),
    )(columns, grads, *(() if blocks is None else (blocks,)))


def branch_products(columns, grad_iso, grad_down, kernel):
    devices, own = columns.shape[:2]
    steps, channels = grad_iso.shape[1:]
    patches = columns[:, :, : 32 * kernel].reshape(devices, own, kernel, 32)[..., :steps]
    down = jnp.einsum("nats,nsb->tab", patches, grad_down, preferred_element_type=FLOAT)
    mine = columns[:, :, 32 * kernel : 32 * kernel + steps]
    shifted = jnp.pad(mine, ((0, 0), (0, 0), (steps - 1, 0)))
    taps = jnp.stack([shifted[:, :, j : j + steps] for j in range(steps)], axis=0)
    iso = jnp.einsum("jnas,nsb->jab", taps, grad_iso, preferred_element_type=FLOAT)
    return (down.reshape(kernel, own * channels), iso.reshape(steps, own * channels))


def body(
    series,
    horizon,
    cotangent,
    fine_down,
    fine_down_bias,
    fine_isometric,
    fine_isometric_bias,
    fine_upsample,
    fine_upsample_bias,
    coarse_down,
    coarse_down_bias,
    coarse_isometric,
    coarse_isometric_bias,
    coarse_upsample,
    coarse_upsample_bias,
    branch_gain,
    branch_bias,
    merge_weight,
    merge_bias,
    first_gain,
    first_bias,
    expand_weight,
    expand_bias,
    reduce_weight,
    reduce_bias,
    final_gain,
    final_bias,
):
    batch_count, length_total, channels = series.shape
    row_count = batch_count * length_total
    devices = lax.axis_size("dp")
    own = channels // devices
    mask_rows = valid_masks(horizon, length_total).reshape(row_count, 1)
    steps = (fine_isometric.shape[0], coarse_isometric.shape[0])
    table = vector_table(
        [
            fine_down_bias,
            fine_isometric_bias,
            fine_upsample_bias,
            coarse_down_bias,
            coarse_isometric_bias,
            coarse_upsample_bias,
            branch_gain,
            branch_bias,
            merge_bias,
            first_gain,
            first_bias,
            reduce_bias,
            final_gain,
            final_bias,
            expand_bias,
        ]
    )
    fine_weights = (fine_down, fine_isometric, fine_upsample)
    coarse_weights = (coarse_down, coarse_isometric, coarse_upsample)
    rows_in = series.reshape(row_count, channels)
    fine_saved = forward_branch(rows_in, table, fine_weights, K_A, steps[0], 0)
    coarse_saved = forward_branch(rows_in, table, coarse_weights, K_B, steps[1], 3)
    columns_fine = exchange(fine_saved[6].reshape(devices, own, -1))
    columns_coarse = exchange(coarse_saved[6].reshape(devices, own, -1))
    merge_matrix = merge_weight.reshape(2 * channels, channels)
    result, grad_branches, dense_rows, vectors = dense_block(
        devices,
        after(fine_saved[0], columns_fine),
        coarse_saved[0],
        merge_matrix,
        expand_weight,
        reduce_weight,
        table,
        mask_rows,
        cotangent.reshape(row_count, channels),
    )
    result = result.reshape(batch_count, length_total, channels)
    known = vectors.shape[0]
    send, right_fine, right_coarse, outer_fine, outer_coarse = outer_grads(
        after(grad_branches, columns_coarse), fine_saved, coarse_saved, table, vectors, devices
    )
    received = exchange(send.reshape(devices, 64, channels))
    part = feed_part(after(dense_rows, send), own)
    pack_fine, down_fine = inner_grads(
        right_fine, fine_saved, table, fine_isometric, fine_upsample
    )
    pack_coarse, down_coarse = inner_grads(
        right_coarse, coarse_saved, table, coarse_isometric, coarse_upsample
    )
    packs = jnp.concatenate([pack_fine, pack_coarse], axis=0)
    packs = after(packs, received)
    down_coarse = after(down_coarse, packs)
    grads = lax.all_gather(packs, "dp", axis=0, tiled=False)
    second = pack_fine.shape[0]
    tap_product = jnp.einsum(
        "nsa,nsb->ab", received[:, :32], received[:, 32:], preferred_element_type=FLOAT
    )
    vector_sum = jnp.sum(received[:, 61:64].astype(FLOAT), axis=(0, 1)).reshape(1, channels)
    high = lax.reduce_precision(vector_sum, 8, 7)
    pair = jnp.concatenate([high, vector_sum - high], axis=0).astype(BFLOAT)
    blocks = jnp.concatenate(
        [
            tap_product.astype(BFLOAT).reshape(devices, own, channels),
            jnp.broadcast_to(pair[None], (devices, 2, channels)),
        ],
        axis=1,
    )
    blocks = exchange(blocks)
    series_gradient = series_grads(
        (down_fine, down_coarse), (outer_fine, outer_coarse), (fine_down, coarse_down)
    )
    part = after(part, series_gradient)
    dense = feed_sums(part, own, expand_weight.shape[1] // devices)
    series_gradient = series_gradient.reshape(series.shape)
    fine_down_gradient, fine_isometric_gradient, fine_sums = weight_grads(
        columns_fine, grads, None, K_A, steps[0], 0, 0
    )
    (
        coarse_down_gradient,
        coarse_isometric_gradient,
        coarse_sums,
        fine_upsample_gradient,
        coarse_upsample_gradient,
    ) = weight_grads(columns_coarse, grads, blocks, K_B, steps[1], 0, second)
    fine_down_bias_gradient, fine_isometric_bias_gradient = fine_sums[0], fine_sums[1]
    coarse_down_bias_gradient, coarse_isometric_bias_gradient = coarse_sums[0], coarse_sums[1]
    inner_sums = jnp.sum(
        grads[:, 2 * steps[0] : 2 * steps[0] + 4].astype(FLOAT)
        + grads[:, second + 2 * steps[1] : second + 2 * steps[1] + 4].astype(FLOAT),
        axis=0,
    )
    inner_sums = jnp.sum(inner_sums.reshape(2, 2, channels), axis=1)
    totals = jnp.sum(blocks[: known + 4, own:].astype(FLOAT), axis=1)
    merge_bias_gradient = totals[0]
    first_gain_gradient = totals[1]
    first_bias_gradient = totals[2]
    reduce_bias_gradient = totals[3]
    final_gain_gradient = totals[4]
    final_bias_gradient = totals[5]
    expand_bias_gradient = totals[6:known].reshape(-1)
    fine_upsample_bias_gradient = totals[known]
    coarse_upsample_bias_gradient = totals[known + 1]
    branch_gain_gradient = totals[known + 2] + inner_sums[0]
    branch_bias_gradient = totals[known + 3] + inner_sums[1]
    merge_weight_gradient, expand_weight_gradient, reduce_weight_gradient = dense
    return (
        result,
        series_gradient,
        fine_down_gradient,
        fine_down_bias_gradient,
        fine_isometric_gradient,
        fine_isometric_bias_gradient,
        fine_upsample_gradient,
        fine_upsample_bias_gradient,
        coarse_down_gradient,
        coarse_down_bias_gradient,
        coarse_isometric_gradient,
        coarse_isometric_bias_gradient,
        coarse_upsample_gradient,
        coarse_upsample_bias_gradient,
        branch_gain_gradient,
        branch_bias_gradient,
        merge_weight_gradient,
        merge_bias_gradient,
        first_gain_gradient,
        first_bias_gradient,
        expand_weight_gradient,
        expand_bias_gradient,
        reduce_weight_gradient,
        reduce_bias_gradient,
        final_gain_gradient,
        final_bias_gradient,
    )


def solution(mesh):
    in_specs = (
        P("dp", None, None),
        P("dp"),
        P("dp", None, None),
        P(),
        P(),
        P(),
        P(),
        P(),
        P(),
        P(),
        P(),
        P(),
        P(),
        P(),
        P(),
        P(),
        P(),
        P(),
        P(),
        P(),
        P(),
        P(),
        P(),
        P(),
        P(),
        P(),
        P(),
    )
    out_specs = (
        P("dp", None, None),
        P("dp", None, None),
        P(None, "dp"),
        P(),
        P(None, "dp"),
        P(),
        P(None, "dp"),
        P(),
        P(None, "dp"),
        P(),
        P(None, "dp"),
        P(),
        P(None, "dp"),
        P(),
        P(),
        P(),
        P(None, "dp"),
        P(),
        P(),
        P(),
        P(None, "dp"),
        P(),
        P("dp", None),
        P(),
        P(),
        P(),
    )
    return jax.shard_map(body, mesh=mesh, in_specs=in_specs, out_specs=out_specs, check_vma=False)
```
